128 devices in a mesh: py: 8 (over x_hi, z), pz: 16 (over x_lo, y, core).
Axes of the slice: x: 4 (x_hi: 2, x_lo: 2; x = x_hi * 2 + x_lo), y: 4, z: 4, core: 2. Of those that a mesh axis runs over, the one named last changes fastest.
Arguments:
- conserved: float32 [5, 512, 256, 256], P(None, 'pz', 'py'), may hold values from -2 to 3.5, as said below
- register: float32 [5, 512, 256, 256], P(None, 'pz', 'py'), may hold values from -6 to 6
- stream_blocks: float32 [2, 3, 128, 128], replicated, may hold values from -0.3125 to 0.3125
- wall_matrix: float32 [256, 256], replicated, may hold values from -0.375 to 0.375
- span_blocks: float32 [16, 3, 32, 32], replicated, may hold values from -0.625 to 0.625
- inflow_gain: float32 [5], replicated, may hold values from 0.5 to 2
- source_block: int32 [128, 1024, 1], replicated, may hold values from 0 to 127; in each aligned block of 1024 rows (0 to 1023, 1024 to 2047, ..., all dimensions but the last counted through in order) at most 16 rows name the same one
- source_column: int32 [128, 1024], replicated, may hold values from 0 to 1023
Outputs:
- new_conserved: float32 [5, 512, 256, 256], P(None, 'pz', 'py')
- new_register: float32 [5, 512, 256, 256], P(None, 'pz', 'py')
The draws below stay inside these ranges and needn't reach their ends.
Inputs may be any that keep to these rules, and one draw needn't show every extreme that they name: Among the 1024 entries of one column block, source_block[b, :, 0], no value appears more than 16 times, and in some column block one value appears exactly 16 times. `conserved`: the first field, the density, lies between 0.5 and 2.
All inputs are finite; a program needn't handle non-finite values.
Results may differ from the reference program's by a relative error of at most 0.0001.
Values sent between devices are 32-bit elements; how exact they have to be, the bound alone decides.
A program may use at most 192 MiB of HBM per device.

```python
import math
import jax
import jax.numpy as jnp
import numpy as np
from jax import lax

FIELDS = 5
NY = 256
NZ = 512
XBL = 128
ZBL = 32
CZ = 32
NX = 256
YROWS = 32
BLK_DEV = 1024
CAP = 16
XREC = 192
NXB = 2
NZB = 16
N_PZ = 16
DEVICES = 128


def draw_conserved(key, part):
    subkeys = jax.random.split(key, 3)
    grid_shape = (NZ, NY, NX)
    density = jax.random.uniform(subkeys[0], grid_shape, jnp.float32, 0.5, 2.0)
    momentum = 0.5 * jnp.clip(jax.random.normal(subkeys[1], (3,) + grid_shape, jnp.float32), -4.0, 4.0)
    energy = jax.random.uniform(subkeys[2], grid_shape, jnp.float32, 2.0, 3.5)
    return jnp.concatenate([density[None], momentum, energy[None]], axis=0)


def set_ends(entries, stream_key, least, top_value):
    extent = entries.shape
    place = [jax.random.randint(jax.random.fold_in(stream_key, axis), (), 0, extent[axis]) for axis in range(len(extent))]
    entries = entries.at[tuple(place)].set(least)
    longest = extent.index(max(extent))
    place[longest] = (place[longest] + 1) % extent[longest]
    return entries.at[tuple(place)].set(top_value)


def block_levels(rng, shape, cuts, low, top_value):
    def one(position, parts):
        draws = jax.random.uniform(jax.random.fold_in(jax.random.fold_in(rng, 6), position), (parts,), jnp.float32, low / len(cuts), top_value / len(cuts))
        return jnp.repeat(jnp.exp(draws), shape[position] // parts).reshape((-1,) + (1,) * (len(shape) - position - 1))

    loudness = one(*cuts[0])
    for cut in cuts[1:]:
        loudness = loudness * one(*cut)
    return loudness


def deal_out(own_key, own, number, rows, count, top, bound, lean):
    ranking = jax.random.permutation(own_key, count)
    heavy_load, usual = portions_of(count, rows * top, bound, lean, True), portions_of(count, rows * top, bound, lean, False)
    places = jnp.arange(count)

    def named(tallies, turn):
        used = int((tallies > 0).sum())
        fixed = max(1, used // 4)
        shifted = fixed + (places - fixed + turn * (used - fixed)) % max(1, count - fixed)
        return jnp.zeros((count,), jnp.int32).at[ranking[jnp.where(places < fixed, places, shifted)]].set(jnp.asarray(tallies, jnp.int32))

    tallies = jnp.where(number % 4 == 0, named(heavy_load, number // 4), named(usual, number - number // 4 - 1))
    mixed = jax.random.permutation(jax.random.fold_in(own, 3), count)
    donor, taker = mixed[0:count // 2 * 2:2], mixed[1:count // 2 * 2:2]
    margin = jnp.minimum(tallies[donor] - 1, bound - tallies[taker]) // 2
    margin = jnp.where((donor == ranking[0]) | (taker == ranking[0]) | (tallies[taker] == 0), 0, jnp.maximum(margin, 0))
    shifted = jax.random.randint(jax.random.fold_in(own, 4), (count // 2,), 0, 1 << 20) % (margin + 1)
    tallies = tallies.at[donor].add(-shifted).at[taker].add(shifted)
    items = jnp.searchsorted(jnp.cumsum(tallies), jnp.arange(rows * top), side="right").astype(jnp.int32)
    table = items.reshape(top, rows).T
    table = table[jax.random.permutation(jax.random.fold_in(own, 1), rows)]
    turn = jax.random.randint(jax.random.fold_in(own, 2), (rows, 1), 0, top)
    return jnp.take_along_axis(table, (jnp.arange(top)[None, :] + turn) % top, axis=1)


def portions_of(amount, total, reach, skew, full):
    weights = [(1 << 20) // math.isqrt(standing ** skew) + 1 for standing in range(1, amount + 1)]
    largest = reach if full else min(reach, max(-(-total // amount), total * weights[0] // sum(weights)))
    least = 1 if total - largest >= amount - 1 else 0
    holding, surplus = [largest] + [least] * (amount - 1), total - largest - least * (amount - 1)
    while surplus > 0:
        candidates = [i for i in range(1, amount) if holding[i] < largest] or [i for i in range(1, amount) if holding[i] < reach]
        whole, left = sum([weights[i] for i in candidates]), surplus
        for i in candidates:
            more = min(reach - holding[i], max(1, left * weights[i] // whole), surplus)
            holding[i] = holding[i] + more
            surplus = surplus - more
    return np.array(holding)


def bell_draw(key, extent, deviation, most, cuts=(), kind=jnp.bfloat16):
    gain = block_levels(key, extent, cuts, -0.22, 0.18) if cuts else 1.0
    result = jax.random.normal(key, extent, jnp.float32) * deviation * gain
    return jnp.minimum(jnp.maximum(result, -most), most).astype(kind)


def setup_inputs(seed: int = 0) -> dict:
    key_of = jax.random.split(jax.random.key(seed), 9)
    conserved = draw_conserved(jax.random.fold_in(key_of[8], 71), 0)
    register = bell_draw(key_of[1], (FIELDS, NZ, NY, NX), 1.0, 6.0, ((1, 16), (2, 8)), jnp.float32)
    stream_blocks = bell_draw(key_of[2], (NXB, 3, XBL, XBL), (3 * XBL) ** -0.5, 0.3125, (), jnp.float32)
    wall_matrix = bell_draw(key_of[3], (NY, NY), NY ** -0.5, 0.375, (), jnp.float32)
    span_blocks = bell_draw(key_of[4], (NZB, 3, ZBL, ZBL), (3 * ZBL) ** -0.5, 0.625, (), jnp.float32)
    inflow_gain = jnp.clip(jnp.exp(jax.random.uniform(key_of[5], (FIELDS,), jnp.float32, math.log(0.5), math.log(2.0))), 0.5, 2.0)
    source_block_keys = jax.random.split(jax.random.fold_in(key_of[6], 1), DEVICES * BLK_DEV // BLK_DEV)
    source_block_turns = jax.random.permutation(jax.random.fold_in(key_of[6], 3), DEVICES * BLK_DEV // BLK_DEV)
    source_block = jax.vmap(lambda own, number: deal_out(jax.random.fold_in(key_of[6], 2), own, number, BLK_DEV, DEVICES, 1, CAP, 2))(source_block_keys, source_block_turns).reshape((DEVICES, BLK_DEV, 1))
    source_column = set_ends(jax.random.randint(key_of[7], (DEVICES, BLK_DEV), 0, BLK_DEV), jax.random.fold_in(key_of[7], 1), 0, BLK_DEV - 1).astype(jnp.int32)
    return {"conserved": conserved, "register": register, "stream_blocks": stream_blocks, "wall_matrix": wall_matrix, "span_blocks": span_blocks, "inflow_gain": inflow_gain, "source_block": source_block, "source_column": source_column}


highest = lax.Precision.HIGHEST
section_decay = -5.0 / 9.0
section_gain = 15.0 / 16.0
time_step = 0.1


def flux_set(values, direction):
    speeds = values[1:4] / values[0]
    pressure = 0.4 * (values[4] - 0.5 * (values[1] * speeds[0] + values[2] * speeds[1] + values[3] * speeds[2]))
    velocity = speeds[direction]
    pieces = [values[1 + direction]]
    for component in range(1, 4):
        moment = values[component] * velocity
        if component - 1 == direction:
            moment = moment + pressure
        pieces.append(moment)
    pieces.append((values[4] + pressure) * velocity)
    return jnp.stack(pieces)


def stream_derivative(values, blocks):
    leading = values.shape[:-1]
    block_count = blocks.shape[0]
    block_width = blocks.shape[2]
    shaped = values.reshape(leading + (block_count, block_width))
    zero_block = jnp.zeros(leading + (1, block_width), jnp.float32)
    padded = jnp.concatenate([zero_block, shaped, zero_block], axis=-2)
    summed = jnp.zeros(leading + (block_count, block_width), jnp.float32)
    for offset in range(3):
        window = padded[..., offset:offset + block_count, :]
        summed = summed + jnp.einsum("kab,...kb->...ka", blocks[:, offset], window, precision=highest)
    return summed.reshape(values.shape)


def wall_derivative(values, matrix):
    return jnp.einsum("ab,fzbx->fzax", matrix, values, precision=highest)


def span_derivative(values, blocks):
    block_count = blocks.shape[0]
    block_width = blocks.shape[2]
    shaped = values.reshape((values.shape[0], block_count, block_width) + values.shape[2:])
    summed = jnp.zeros(shaped.shape, jnp.float32)
    for offset in range(3):
        rolled = jnp.roll(shaped, 1 - offset, axis=1)
        summed = summed + jnp.einsum("kab,fkbyx->fkayx", blocks[:, offset], rolled, precision=highest)
    return summed.reshape(values.shape)


def reference(conserved, register, stream_blocks, wall_matrix, span_blocks, inflow_gain, source_block, source_column):
    block_ids = jnp.arange(DEVICES, dtype=jnp.int32)[:, None]
    columns = jnp.arange(BLK_DEV, dtype=jnp.int32)[None, :]
    target_span = (block_ids % N_PZ) * CZ + columns // YROWS
    target_wall = (block_ids // N_PZ) * YROWS + columns % YROWS
    anchor = source_block[:, :, 0]
    anchor_span = (anchor % N_PZ) * CZ + source_column // YROWS
    anchor_wall = (anchor // N_PZ) * YROWS + source_column % YROWS
    recycle = conserved[:, :, :, XREC]
    fetched = recycle[:, anchor_span, anchor_wall] * inflow_gain[:, None, None]
    inlet_plane = jnp.zeros_like(recycle).at[:, target_span, target_wall].set(fetched)
    current = conserved.at[:, :, :, 0].set(inlet_plane)
    stream_term = stream_derivative(flux_set(current, 0), stream_blocks)
    wall_term = wall_derivative(flux_set(current, 1), wall_matrix)
    span_term = span_derivative(flux_set(current, 2), span_blocks)
    new_register = section_decay * register - time_step * (stream_term + wall_term + span_term)
    new_conserved = current + section_gain * new_register
    return new_conserved, new_register
```

```python
import functools

import jax
import jax.numpy as jnp
from jax import lax
from jax.experimental import pallas as pl
from jax.experimental.pallas import tpu as pltpu
from jax.sharding import PartitionSpec as P

MESH = pl.DeviceIdType.MESH
F32 = jnp.float32
BF16 = jnp.bfloat16
SECTION_DECAY = -5.0 / 9.0
SECTION_GAIN = 15.0 / 16.0
TIME_STEP = 0.1
ORDER = (4, 1, 3, 5, 7, 6, 2)


def flux(direction, density, first, second, third, energy):
    inverse = 1.0 / density
    moments = (first, second, third)
    speeds = tuple(moment * inverse for moment in moments)
    pressure = 0.4 * (
        energy - 0.5 * (first * speeds[0] + second * speeds[1] + third * speeds[2])
    )
    velocity = speeds[direction]
    pieces = [moments[direction]]
    for component in range(3):
        moment = moments[component] * velocity
        if component == direction:
            moment = moment + pressure
        pieces.append(moment)
    pieces.append((energy + pressure) * velocity)
    return pieces


def halves(value):
    high = value.astype(BF16)
    return high, (value - high.astype(F32)).astype(BF16)


def thirds(value):
    high = value.astype(BF16)
    rest = value - high.astype(F32)
    middle = rest.astype(BF16)
    return high, middle, (rest - middle.astype(F32)).astype(BF16)


def mm(left, right):
    return jnp.dot(left, right, preferred_element_type=F32)


def iota(shape, axis):
    return lax.broadcasted_iota(jnp.int32, shape, axis)


def kernel(
    con,
    reg,
    stream_in,
    wall_in,
    span_in,
    gain,
    source_block,
    source_column,
    out_con,
    out_reg,
    cur,
    got,
    wall_out,
    back,
    base,
    halo,
    work,
    stream_work,
    wall_w,
    stream_w,
    span_w,
    slot_key,
    picked,
    staged,
    received,
    load_sem,
    fs,
    fr,
    bs,
    br,
    hs,
    hr,
    s1s,
    s1r,
    s2s,
    s2r,
    out_sem,
):
    py, pz = lax.axis_index("py"), lax.axis_index("pz")
    me = py * 16 + pz

    def peer(offset):
        return lax.rem(py // 4 + offset // 4, 2) * 4 + lax.rem(lax.rem(py, 4) + offset % 4, 4)

    def half(h):
        return pl.ds(128 * h, 128)

    def remote(src, dst, send, recv, device):
        return pltpu.make_async_remote_copy(
            src_ref=src,
            dst_ref=dst,
            send_sem=send,
            recv_sem=recv,
            device_id=device,
            device_id_type=MESH,
        )

    def forward(h, q, offset):
        p = peer(offset)
        src = con.at[:, p, q, :, half(1)] if h == 1 else cur.at[0, :, p, q]
        return remote(
            src, got.at[h, q, :, py], fs.at[h, q, offset], fr.at[h, q, offset], (p, pz)
        )

    def own(h, q):
        src = con.at[:, py, q, :, half(1)] if h == 1 else cur.at[0, :, py, q]
        return pltpu.make_async_copy(src, got.at[h, q, :, py], fr.at[h, q, 0])

    def giveback(h, q, offset):
        p = peer(offset)
        return remote(
            wall_out.at[h, q, :, p],
            back.at[h, :, py, q],
            bs.at[h, q, offset],
            br.at[h, q, offset],
            (p, pz),
        )

    def beside(h, side, i):
        rows = pl.ds(2 * i, 2)
        src = con.at[:, rows, :, :, half(1)] if h == 1 else cur.at[0, :, rows]
        target = lax.rem(pz + (1 if side == 0 else 15), 16)
        return remote(
            src, halo.at[side, h, :, rows], hs.at[h, side, i], hr.at[h, side, i], (py, target)
        )

    def send_forward(h, q):
        own(h, q).start()
        for offset in ORDER:
            forward(h, q, offset).start()

    def send_beside(h, i):
        for side in range(2):
            beside(h, side, i).start()

    def stage_one(offset):
        p = peer(offset)
        return remote(
            picked.at[p], staged.at[:, py], s1s.at[offset], s1r.at[offset], (p, pz)
        )

    def stage_two(offset):
        target = lax.rem(pz + offset, 16)
        return remote(
            staged.at[target], received.at[pz], s2s.at[offset], s2r.at[offset], (py, target)
        )

    loads = [
        pltpu.make_async_copy(con.at[:, :, :, :, half(h)], cur.at[h], load_sem.at[h])
        for h in (1, 0)
    ] + [
        pltpu.make_async_copy(reg.at[:, :, :, :, half(h)], base.at[h], load_sem.at[2 + h])
        for h in range(2)
    ]
    for load in loads:
        load.start()

    barrier = pltpu.get_barrier_semaphore()
    for offset in range(1, 8):
        pl.semaphore_signal(barrier, inc=1, device_id=(peer(offset), pz), device_id_type=MESH)
    for offset in range(1, 16):
        pl.semaphore_signal(
            barrier, inc=1, device_id=(py, lax.rem(pz + offset, 16)), device_id_type=MESH
        )
    pl.semaphore_wait(barrier, 22)

    send_forward(1, 0)
    send_beside(1, 0)
    send_forward(1, 1)

    lane = iota((128, 128), 1)
    row = iota((128, 128), 0)
    strict = jnp.where(row < lane, 1.0, 0.0).astype(BF16)
    counts = jnp.concatenate([strict, jnp.ones((128, 128), BF16)], axis=1)
    passed = jnp.zeros((128, 128), F32)
    for g in range(8):
        mine = source_block[:, 128 * g : 128 * g + 128] == me
        ranked = mm(jnp.where(mine, 1.0, 0.0).astype(BF16), counts)
        slot_key[:, 128 * g : 128 * g + 128] = jnp.where(mine, ranked[:, :128] + passed, -1.0)
        passed = passed + ranked[:, 128:]

    loads[0].wait()
    for g in range(8):
        plane = jnp.zeros((128, 128), F32)
        for f in range(5):
            value = cur[1, f, g].reshape(128, 128)
            plane = plane + jnp.where(
                lane == f, jnp.broadcast_to(value[:, 64:65], (128, 128)), 0.0
            )
        for part, piece in enumerate(thirds(plane)):
            work[pl.ds(128 * g, 128), 128 * part : 128 * part + 128] = piece

    def pick(r, carry):
        total = jnp.zeros((128, 128), F32)
        for g in range(8):
            columns = source_column[:, 128 * g : 128 * g + 128].astype(F32)
            total = total + jnp.where(
                slot_key[:, 128 * g : 128 * g + 128] == r.astype(F32), columns, 0.0
            )
        wanted = jnp.sum(total, axis=1, keepdims=True)
        choose = jnp.concatenate(
            [
                jnp.where((lane + 128 * g).astype(F32) == wanted, 1.0, 0.0).astype(BF16)
                for g in range(8)
            ],
            axis=1,
        )
        values = mm(choose, work[pl.ds(0, 1024), 0:384])
        values = values[:, :128] + values[:, 128:256] + values[:, 256:384]
        return carry + pltpu.roll(values, 8 * r, 1)

    picked[...] = lax.fori_loop(0, 16, pick, jnp.zeros((128, 128), F32)).reshape(8, 16, 128)

    for offset in range(1, 8):
        stage_one(offset).start()
    for p in range(8):

        @pl.when(py == p)
        def _(p=p):
            staged[:, p, :] = picked[p]

    send_forward(1, 2)
    send_beside(1, 1)

    high, low = halves(wall_in[...])
    wall_w[:, 0:256] = high
    wall_w[:, 256:512] = high
    wall_w[:, 512:768] = low
    for k in range(2):
        for j in range(2):
            high, low = halves(stream_in[k, j - k + 1])
            rows = slice(128 * k, 128 * k + 128)
            stream_w[rows, 128 * j : 128 * j + 128] = high
            stream_w[rows, 256 + 128 * j : 256 + 128 * j + 128] = high
            stream_w[rows, 512 + 128 * j : 512 + 128 * j + 128] = low
    spread = jnp.where(iota((256, 32), 0) // 8 == iota((256, 32), 1), 1.0, 0.0).astype(BF16)
    aligned = lax.rem(iota((256, 256), 0), 8) == lax.rem(iota((256, 256), 1), 8)
    for j in range(3):
        for part, piece in enumerate(halves(span_in[pz, j])):
            wide = mm(spread, piece).astype(BF16)
            full = lax.dot_general(
                wide, spread, (((1,), (1,)), ((), ())), preferred_element_type=F32
            )
            full = jnp.where(aligned, full, 0.0).astype(BF16)
            if part == 0:
                span_w[:, 256 * j : 256 * j + 256] = full
                span_w[:, 768 + 256 * j : 768 + 256 * j + 256] = full
            else:
                span_w[:, 1536 + 256 * j : 1536 + 256 * j + 256] = full

    for offset in range(1, 8):
        stage_one(offset).wait_recv()
    for offset in range(1, 16):
        stage_two(offset).start()
    for p in range(16):

        @pl.when(pz == p)
        def _(p=p):
            received[p] = staged[p]

    send_forward(1, 3)
    send_beside(1, 2)
    send_beside(1, 3)
    loads[1].wait()
    for offset in range(1, 16):
        stage_two(offset).wait_recv()

    arrived = jnp.concatenate(thirds(received[...].reshape(128, 128)), axis=1)
    below = jnp.where(lane < row, 1.0, 0.0).astype(BF16)
    before = jnp.zeros((1, 128), F32)
    sources = source_block[pl.ds(me, 1), :]
    sources = ((sources & 15) * 8 + (sources >> 4)).astype(F32)
    for g in range(8):
        named = jnp.broadcast_to(sources[:, 128 * g : 128 * g + 128], (128, 128)).T
        flags = jnp.where(named == lane.astype(F32), 1.0, 0.0)
        ahead = mm(below, flags.astype(BF16)) + before
        before = before + jnp.sum(flags, axis=0, keepdims=True)
        rank = jnp.sum(flags * ahead, axis=1, keepdims=True)
        values = mm(flags.astype(BF16), arrived)
        values = values[:, :128] + values[:, 128:256] + values[:, 256:384]
        values = jnp.where((lane // 8).astype(F32) == rank, values, 0.0)
        for shift in (64, 32, 16, 8):
            values = values + pltpu.roll(values, shift, 1)
        for f in range(5):
            column = jnp.broadcast_to(values[:, f : f + 1] * gain[f], (128, 128))
            old = cur[0, f, g].reshape(128, 128)
            cur[0, f, g] = jnp.where(lane == 0, column, old).reshape(4, 32, 128)

    for q in range(4):
        send_forward(0, q)
        send_beside(0, q)

    loads[2].wait()
    loads[3].wait()

    def stream(p, carry):
        for q in range(4):
            for h in range(2):
                pieces = flux(0, *[cur[h, f, p, q] for f in range(5)])
                for f in range(5):
                    high, low = halves(pieces[f])
                    rows = pl.ds(128 * f + 32 * q, 32)
                    stream_work[rows, 128 * h : 128 * h + 128] = high
                    stream_work[rows, 256 + 128 * h : 384 + 128 * h] = low
        nt = (((1,), (1,)), ((), ()))
        term = lax.dot_general(
            stream_work[...], stream_w[:, 0:512], nt, preferred_element_type=F32
        ) + lax.dot_general(
            stream_work[:, 0:256], stream_w[:, 512:768], nt, preferred_element_type=F32
        )
        for f in range(5):
            for h in range(2):
                part = term[128 * f : 128 * f + 128, 128 * h : 128 * h + 128]
                base[h, f, p] = SECTION_DECAY * base[h, f, p] - TIME_STEP * part.reshape(
                    4, 32, 128
                )
        return carry

    lax.fori_loop(0, 8, stream, 0)

    def wall(h, q):
        own(h, q).wait()
        for offset in range(1, 8):
            forward(h, q, offset).wait_recv()

        def fill(s, carry):
            pieces = flux(1, *[got[h, q, f, s] for f in range(5)])
            for f in range(5):
                high, low = halves(pieces[f])
                work[pl.ds(32 * s, 32), 128 * f : 128 * f + 128] = high
                work[pl.ds(256 + 32 * s, 32), 128 * f : 128 * f + 128] = low
            return carry

        lax.fori_loop(0, 8, fill, 0)
        term = mm(wall_w[:, 0:512], work[pl.ds(0, 512), :]) + mm(
            wall_w[:, 512:768], work[pl.ds(0, 256), :]
        )
        for f in range(5):
            wall_out[h, q, f] = term[:, 128 * f : 128 * f + 128].reshape(8, 32, 128)
        for offset in ORDER:
            giveback(h, q, offset).start()
        for f in range(5):
            back[h, f, py, q] = wall_out[h, q, f, py]

    def span(h):
        for side in range(2):
            for i in range(4):
                beside(h, side, i).wait_recv()

        def tile(t, carry):
            rows = pl.ds(pl.multiple_of(8 * t, 8), 8)

            def fill(p, inner):
                for j in range(3):
                    if j == 1:
                        fields = [cur[h, f, p, :, rows, :] for f in range(5)]
                    else:
                        fields = [halo[j // 2, h, f, p, :, rows, :] for f in range(5)]
                    pieces = flux(2, *[field.reshape(32, 128) for field in fields])
                    for f in range(5):
                        high, low = halves(pieces[f])
                        work[pl.ds(256 * j + 32 * p, 32), 128 * f : 128 * f + 128] = high
                        work[pl.ds(768 + 256 * j + 32 * p, 32), 128 * f : 128 * f + 128] = low
                return inner

            lax.fori_loop(0, 8, fill, 0)
            term = mm(span_w[:, 0:1536], work[...]) + mm(
                span_w[:, 1536:2304], work[pl.ds(0, 768), :]
            )
            for f in range(5):
                part = term[:, 128 * f : 128 * f + 128].reshape(8, 4, 8, 128)
                base[h, f, :, :, rows, :] = base[h, f, :, :, rows, :] - TIME_STEP * part
            return carry

        lax.fori_loop(0, 4, tile, 0)

    def outputs(h, q):
        return (
            pltpu.make_async_copy(
                base.at[h, :, :, q], out_reg.at[:, :, q, :, half(h)], out_sem.at[0, h, q]
            ),
            pltpu.make_async_copy(
                got.at[h, q], out_con.at[:, :, q, :, half(h)], out_sem.at[1, h, q]
            ),
        )

    def finish(h, q):
        for offset in range(1, 8):
            giveback(h, q, offset).wait_recv()

        def join(p, carry):
            for f in range(5):
                fresh = base[h, f, p, q] - TIME_STEP * back[h, f, p, q]
                base[h, f, p, q] = fresh
                got[h, q, f, p] = cur[h, f, p, q] + SECTION_GAIN * fresh
            return carry

        lax.fori_loop(0, 8, join, 0)
        for copy in outputs(h, q):
            copy.start()

    for q in range(4):
        wall(1, q)
    span(1)
    for q in range(4):
        wall(0, q)
    span(0)
    for h in (1, 0):
        for q in range(4):
            finish(h, q)

    for offset in range(1, 8):
        stage_one(offset).wait_send()
    for offset in range(1, 16):
        stage_two(offset).wait_send()
    for h in (1, 0):
        for q in range(4):
            for offset in range(1, 8):
                forward(h, q, offset).wait_send()
                giveback(h, q, offset).wait_send()
            for side in range(2):
                beside(h, side, q).wait_send()
            for copy in outputs(h, q):
                copy.wait()


def local(
    conserved,
    register,
    stream_blocks,
    wall_matrix,
    span_blocks,
    inflow_gain,
    source_block,
    source_column,
):
    shape = (5, 8, 4, 32, 256)
    anywhere = pl.BlockSpec(memory_space=pl.ANY)
    vmem = pl.BlockSpec(memory_space=pltpu.VMEM)
    dma = pltpu.SemaphoreType.DMA
    halved = (2, 5, 8, 4, 32, 128)
    new_conserved, new_register = pl.pallas_call(
        kernel,
        out_shape=[jax.ShapeDtypeStruct(shape, F32)] * 2,
        in_specs=[
            anywhere,
            anywhere,
            vmem,
            vmem,
            vmem,
            pl.BlockSpec(memory_space=pltpu.SMEM),
            vmem,
            vmem,
        ],
        out_specs=[anywhere, anywhere],
        scratch_shapes=[
            pltpu.VMEM(halved, F32),
            pltpu.VMEM((2, 4, 5, 8, 32, 128), F32),
            pltpu.VMEM((2, 4, 5, 8, 32, 128), F32),
            pltpu.VMEM(halved, F32),
            pltpu.VMEM(halved, F32),
            pltpu.VMEM((2,) + halved, F32),
            pltpu.VMEM((1536, 640), BF16),
            pltpu.VMEM((640, 512), BF16),
            pltpu.VMEM((256, 768), BF16),
            pltpu.VMEM((256, 768), BF16),
            pltpu.VMEM((256, 2304), BF16),
            pltpu.VMEM((128, 1024), F32),
            pltpu.VMEM((8, 16, 128), F32),
            pltpu.VMEM((16, 8, 128), F32),
            pltpu.VMEM((16, 8, 128), F32),
            dma((4,)),
            dma((2, 4, 8)),
            dma((2, 4, 8)),
            dma((2, 4, 8)),
            dma((2, 4, 8)),
            dma((2, 2, 4)),
            dma((2, 2, 4)),
            dma((8,)),
            dma((8,)),
            dma((16,)),
            dma((16,)),
            dma((2, 2, 4)),
        ],
        compiler_params=pltpu.CompilerParams(
            collective_id=0, has_side_effects=True, vmem_limit_bytes=60 * 2**20
        ),
        name="section",
    )(
        conserved.reshape(shape),
        register.reshape(shape),
        stream_blocks,
        wall_matrix,
        span_blocks,
        inflow_gain,
        source_block.reshape(128, 1024),
        source_column,
    )
    return new_conserved.reshape(conserved.shape), new_register.reshape(register.shape)


def solution(mesh):
    split = P(None, "pz", "py", None)
    return jax.shard_map(
        local,
        mesh=mesh,
        in_specs=(split, split, P(), P(), P(), P(), P(), P()),
        out_specs=(split, split),
        check_vma=False,
    )
```

```python
import functools

import jax
import jax.numpy as jnp
from jax import lax
from jax.experimental import pallas as pl
from jax.experimental.pallas import tpu as pltpu
from jax.sharding import PartitionSpec as P

MESH = pl.DeviceIdType.MESH
F32 = jnp.float32
BF16 = jnp.bfloat16
SECTION_DECAY = -5.0 / 9.0
SECTION_GAIN = 15.0 / 16.0
TIME_STEP = 0.1
ORDER = (4, 1, 3, 5, 7, 6, 2)
RELAYED = 2


def flux(direction, density, first, second, third, energy):
    inverse = 1.0 / density
    moments = (first, second, third)
    speeds = tuple(moment * inverse for moment in moments)
    pressure = 0.4 * (
        energy - 0.5 * (first * speeds[0] + second * speeds[1] + third * speeds[2])
    )
    velocity = speeds[direction]
    pieces = [moments[direction]]
    for component in range(3):
        moment = moments[component] * velocity
        if component == direction:
            moment = moment + pressure
        pieces.append(moment)
    pieces.append((energy + pressure) * velocity)
    return pieces


def halves(value):
    high = value.astype(BF16)
    return high, (value - high.astype(F32)).astype(BF16)


def thirds(value):
    high = value.astype(BF16)
    rest = value - high.astype(F32)
    middle = rest.astype(BF16)
    return high, middle, (rest - middle.astype(F32)).astype(BF16)


def mm(left, right):
    return jnp.dot(left, right, preferred_element_type=F32)


def iota(shape, axis):
    return lax.broadcasted_iota(jnp.int32, shape, axis)


def kernel(
    con,
    reg,
    stream_in,
    wall_in,
    span_in,
    gain,
    source_block,
    source_column,
    out_con,
    out_reg,
    cur,
    got,
    wall_out,
    back,
    base,
    halo,
    hop,
    work,
    stream_work,
    wall_w,
    stream_w,
    span_w,
    slot_key,
    picked,
    staged,
    received,
    load_sem,
    fs,
    fr,
    bs,
    br,
    hs,
    hr,
    ps,
    pr,
    s1s,
    s1r,
    s2s,
    s2r,
    out_sem,
):
    py, pz = lax.axis_index("py"), lax.axis_index("pz")
    me = py * 16 + pz

    def peer(offset):
        return lax.rem(py // 4 + offset // 4, 2) * 4 + lax.rem(lax.rem(py, 4) + offset % 4, 4)

    def half(h):
        return pl.ds(128 * h, 128)

    def remote(src, dst, send, recv, device):
        return pltpu.make_async_remote_copy(
            src_ref=src,
            dst_ref=dst,
            send_sem=send,
            recv_sem=recv,
            device_id=device,
            device_id_type=MESH,
        )

    def forward(h, q, offset):
        p = peer(offset)
        src = con.at[:, p, q, :, half(1)] if h == 1 else cur.at[0, :, p, q]
        return remote(
            src, got.at[h, q, :, py], fs.at[h, q, offset], fr.at[h, q, offset], (p, pz)
        )

    def own(h, q):
        src = con.at[:, py, q, :, half(1)] if h == 1 else cur.at[0, :, py, q]
        return pltpu.make_async_copy(src, got.at[h, q, :, py], fr.at[h, q, 0])

    def giveback(h, q, offset):
        p = peer(offset)
        return remote(
            wall_out.at[h, q, :, p],
            back.at[h, :, py, q],
            bs.at[h, q, offset],
            br.at[h, q, offset],
            (p, pz),
        )

    def beside(h, side, i):
        rows = pl.ds(2 * i, 2)
        src = con.at[:, rows, :, :, half(1)] if h == 1 else cur.at[0, :, rows]
        target = lax.rem(pz + (1 if side == 0 else 15), 16)
        return remote(
            src, halo.at[side, h, :, rows], hs.at[h, side, i], hr.at[h, side, i], (py, target)
        )

    def passing(h, side, i):
        rows = pl.ds(2 * i, 2)
        src = con.at[:, rows, :, :, half(1)] if h == 1 else cur.at[0, :, rows]
        target = lax.rem(pz + (14 if side == 0 else 2), 16)
        return remote(src, hop.at[h, i], hs.at[h, side, i], pr.at[h, i], (py, target))

    def onward(h, side, i):
        target = lax.rem(pz + (3 if side == 0 else 13), 16)
        return remote(
            hop.at[h, i],
            halo.at[side, h, :, pl.ds(2 * i, 2)],
            ps.at[h, i],
            hr.at[h, side, i],
            (py, target),
        )

    wraps = [lax.rem(pz, 8) == 7, lax.rem(pz, 8) == 0]
    relays = [lax.rem(pz, 8) == 5, lax.rem(pz, 8) == 2]

    def send_onward(h, i):
        for side in range(2):

            @pl.when(relays[side])
            def _(side=side):
                passing(h, side, i).wait_recv()
                onward(h, side, i).start()

    def send_forward(h, q):
        own(h, q).start()
        for offset in ORDER:
            forward(h, q, offset).start()

    def send_beside(h, i):
        for side in range(2):
            if i < RELAYED:

                @pl.when(wraps[side])
                def _(side=side):
                    passing(h, side, i).start()

                @pl.when(jnp.logical_not(wraps[side]))
                def _(side=side):
                    beside(h, side, i).start()

            else:
                beside(h, side, i).start()

    def stage_one(offset):
        p = peer(offset)
        return remote(
            picked.at[p], staged.at[:, py], s1s.at[offset], s1r.at[offset], (p, pz)
        )

    def stage_two(offset):
        target = lax.rem(pz + offset, 16)
        return remote(
            staged.at[target], received.at[pz], s2s.at[offset], s2r.at[offset], (py, target)
        )

    loads = [
        pltpu.make_async_copy(con.at[:, :, :, :, half(h)], cur.at[h], load_sem.at[h])
        for h in (1, 0)
    ] + [
        pltpu.make_async_copy(reg.at[:, :, :, :, half(h)], base.at[h], load_sem.at[2 + h])
        for h in range(2)
    ]
    for load in loads:
        load.start()

    barrier = pltpu.get_barrier_semaphore()
    for offset in range(1, 8):
        pl.semaphore_signal(barrier, inc=1, device_id=(peer(offset), pz), device_id_type=MESH)
    for offset in range(1, 16):
        pl.semaphore_signal(
            barrier, inc=1, device_id=(py, lax.rem(pz + offset, 16)), device_id_type=MESH
        )
    pl.semaphore_wait(barrier, 22)

    send_beside(1, 0)
    send_forward(1, 0)
    send_beside(1, 1)
    send_forward(1, 1)

    lane = iota((128, 128), 1)
    row = iota((128, 128), 0)
    strict = jnp.where(row < lane, 1.0, 0.0).astype(BF16)
    counts = jnp.concatenate([strict, jnp.ones((128, 128), BF16)], axis=1)
    passed = jnp.zeros((128, 128), F32)
    for g in range(8):
        mine = source_block[:, 128 * g : 128 * g + 128] == me
        ranked = mm(jnp.where(mine, 1.0, 0.0).astype(BF16), counts)
        slot_key[:, 128 * g : 128 * g + 128] = jnp.where(mine, ranked[:, :128] + passed, -1.0)
        passed = passed + ranked[:, 128:]

    loads[0].wait()
    for g in range(8):
        plane = jnp.zeros((128, 128), F32)
        for f in range(5):
            value = cur[1, f, g].reshape(128, 128)
            plane = plane + jnp.where(
                lane == f, jnp.broadcast_to(value[:, 64:65], (128, 128)), 0.0
            )
        for part, piece in enumerate(thirds(plane)):
            work[pl.ds(128 * g, 128), 128 * part : 128 * part + 128] = piece

    def pick(r, carry):
        total = jnp.zeros((128, 128), F32)
        for g in range(8):
            columns = source_column[:, 128 * g : 128 * g + 128].astype(F32)
            total = total + jnp.where(
                slot_key[:, 128 * g : 128 * g + 128] == r.astype(F32), columns, 0.0
            )
        wanted = jnp.sum(total, axis=1, keepdims=True)
        choose = jnp.concatenate(
            [
                jnp.where((lane + 128 * g).astype(F32) == wanted, 1.0, 0.0).astype(BF16)
                for g in range(8)
            ],
            axis=1,
        )
        values = mm(choose, work[pl.ds(0, 1024), 0:384])
        values = values[:, :128] + values[:, 128:256] + values[:, 256:384]
        return carry + pltpu.roll(values, 8 * r, 1)

    picked[...] = lax.fori_loop(0, 16, pick, jnp.zeros((128, 128), F32)).reshape(8, 16, 128)

    for offset in range(1, 8):
        stage_one(offset).start()
    for p in range(8):

        @pl.when(py == p)
        def _(p=p):
            staged[:, p, :] = picked[p]

    send_onward(1, 0)
    send_forward(1, 2)
    send_beside(1, 2)

    high, low = halves(wall_in[...])
    wall_w[:, 0:256] = high
    wall_w[:, 256:512] = high
    wall_w[:, 512:768] = low
    for k in range(2):
        for j in range(2):
            high, low = halves(stream_in[k, j - k + 1])
            rows = slice(128 * k, 128 * k + 128)
            stream_w[rows, 128 * j : 128 * j + 128] = high
            stream_w[rows, 256 + 128 * j : 256 + 128 * j + 128] = high
            stream_w[rows, 512 + 128 * j : 512 + 128 * j + 128] = low
    spread = jnp.where(iota((256, 32), 0) // 8 == iota((256, 32), 1), 1.0, 0.0).astype(BF16)
    aligned = lax.rem(iota((256, 256), 0), 8) == lax.rem(iota((256, 256), 1), 8)
    for j in range(3):
        for part, piece in enumerate(halves(span_in[pz, j])):
            wide = mm(spread, piece).astype(BF16)
            full = lax.dot_general(
                wide, spread, (((1,), (1,)), ((), ())), preferred_element_type=F32
            )
            full = jnp.where(aligned, full, 0.0).astype(BF16)
            if part == 0:
                span_w[:, 256 * j : 256 * j + 256] = full
                span_w[:, 768 + 256 * j : 768 + 256 * j + 256] = full
            else:
                span_w[:, 1536 + 256 * j : 1536 + 256 * j + 256] = full

    for offset in range(1, 8):
        stage_one(offset).wait_recv()
    for offset in range(1, 16):
        stage_two(offset).start()
    for p in range(16):

        @pl.when(pz == p)
        def _(p=p):
            received[p] = staged[p]

    send_onward(1, 1)
    send_forward(1, 3)
    send_beside(1, 3)
    loads[1].wait()
    for offset in range(1, 16):
        stage_two(offset).wait_recv()

    arrived = jnp.concatenate(thirds(received[...].reshape(128, 128)), axis=1)
    below = jnp.where(lane < row, 1.0, 0.0).astype(BF16)
    before = jnp.zeros((1, 128), F32)
    sources = source_block[pl.ds(me, 1), :]
    sources = ((sources & 15) * 8 + (sources >> 4)).astype(F32)
    for g in range(8):
        named = jnp.broadcast_to(sources[:, 128 * g : 128 * g + 128], (128, 128)).T
        flags = jnp.where(named == lane.astype(F32), 1.0, 0.0)
        ahead = mm(below, flags.astype(BF16)) + before
        before = before + jnp.sum(flags, axis=0, keepdims=True)
        rank = jnp.sum(flags * ahead, axis=1, keepdims=True)
        values = mm(flags.astype(BF16), arrived)
        values = values[:, :128] + values[:, 128:256] + values[:, 256:384]
        values = jnp.where((lane // 8).astype(F32) == rank, values, 0.0)
        for shift in (64, 32, 16, 8):
            values = values + pltpu.roll(values, shift, 1)
        for f in range(5):
            column = jnp.broadcast_to(values[:, f : f + 1] * gain[f], (128, 128))
            old = cur[0, f, g].reshape(128, 128)
            cur[0, f, g] = jnp.where(lane == 0, column, old).reshape(4, 32, 128)

    for q in range(4):
        send_beside(0, q)
        send_forward(0, q)

    loads[2].wait()
    loads[3].wait()

    def stream(p, carry):
        for q in range(4):
            for h in range(2):
                pieces = flux(0, *[cur[h, f, p, q] for f in range(5)])
                for f in range(5):
                    high, low = halves(pieces[f])
                    rows = pl.ds(128 * f + 32 * q, 32)
                    stream_work[rows, 128 * h : 128 * h + 128] = high
                    stream_work[rows, 256 + 128 * h : 384 + 128 * h] = low
        nt = (((1,), (1,)), ((), ()))
        term = lax.dot_general(
            stream_work[...], stream_w[:, 0:512], nt, preferred_element_type=F32
        ) + lax.dot_general(
            stream_work[:, 0:256], stream_w[:, 512:768], nt, preferred_element_type=F32
        )
        for f in range(5):
            for h in range(2):
                part = term[128 * f : 128 * f + 128, 128 * h : 128 * h + 128]
                base[h, f, p] = SECTION_DECAY * base[h, f, p] - TIME_STEP * part.reshape(
                    4, 32, 128
                )
        return carry

    lax.fori_loop(0, 8, stream, 0)
    for i in range(RELAYED):
        send_onward(0, i)

    def wall(h, q):
        own(h, q).wait()
        for offset in range(1, 8):
            forward(h, q, offset).wait_recv()

        def fill(s, carry):
            pieces = flux(1, *[got[h, q, f, s] for f in range(5)])
            for f in range(5):
                high, low = halves(pieces[f])
                work[pl.ds(32 * s, 32), 128 * f : 128 * f + 128] = high
                work[pl.ds(256 + 32 * s, 32), 128 * f : 128 * f + 128] = low
            return carry

        lax.fori_loop(0, 8, fill, 0)
        term = mm(wall_w[:, 0:512], work[pl.ds(0, 512), :]) + mm(
            wall_w[:, 512:768], work[pl.ds(0, 256), :]
        )
        for f in range(5):
            wall_out[h, q, f] = term[:, 128 * f : 128 * f + 128].reshape(8, 32, 128)
        for offset in ORDER:
            giveback(h, q, offset).start()
        for f in range(5):
            back[h, f, py, q] = wall_out[h, q, f, py]

    def span(h):
        for side in range(2):
            for i in range(4):
                beside(h, side, i).wait_recv()

        def tile(t, carry):
            rows = pl.ds(pl.multiple_of(8 * t, 8), 8)

            def fill(p, inner):
                for j in range(3):
                    if j == 1:
                        fields = [cur[h, f, p, :, rows, :] for f in range(5)]
                    else:
                        fields = [halo[j // 2, h, f, p, :, rows, :] for f in range(5)]
                    pieces = flux(2, *[field.reshape(32, 128) for field in fields])
                    for f in range(5):
                        high, low = halves(pieces[f])
                        work[pl.ds(256 * j + 32 * p, 32), 128 * f : 128 * f + 128] = high
                        work[pl.ds(768 + 256 * j + 32 * p, 32), 128 * f : 128 * f + 128] = low
                return inner

            lax.fori_loop(0, 8, fill, 0)
            term = mm(span_w[:, 0:1536], work[...]) + mm(
                span_w[:, 1536:2304], work[pl.ds(0, 768), :]
            )
            for f in range(5):
                part = term[:, 128 * f : 128 * f + 128].reshape(8, 4, 8, 128)
                base[h, f, :, :, rows, :] = base[h, f, :, :, rows, :] - TIME_STEP * part
            return carry

        lax.fori_loop(0, 4, tile, 0)

    def outputs(h, q):
        return (
            pltpu.make_async_copy(
                base.at[h, :, :, q], out_reg.at[:, :, q, :, half(h)], out_sem.at[0, h, q]
            ),
            pltpu.make_async_copy(
                got.at[h, q], out_con.at[:, :, q, :, half(h)], out_sem.at[1, h, q]
            ),
        )

    def finish(h, q):
        for offset in range(1, 8):
            giveback(h, q, offset).wait_recv()

        def join(p, carry):
            for f in range(5):
                fresh = base[h, f, p, q] - TIME_STEP * back[h, f, p, q]
                base[h, f, p, q] = fresh
                got[h, q, f, p] = cur[h, f, p, q] + SECTION_GAIN * fresh
            return carry

        lax.fori_loop(0, 8, join, 0)
        for copy in outputs(h, q):
            copy.start()

    for q in range(4):
        wall(1, q)
    span(1)
    for q in range(4):
        wall(0, q)
    span(0)
    for h in (1, 0):
        for q in range(4):
            finish(h, q)

    for offset in range(1, 8):
        stage_one(offset).wait_send()
    for offset in range(1, 16):
        stage_two(offset).wait_send()
    for h in (1, 0):
        for q in range(4):
            for offset in range(1, 8):
                forward(h, q, offset).wait_send()
                giveback(h, q, offset).wait_send()
            for side in range(2):
                beside(h, side, q).wait_send()
                if q < RELAYED:

                    @pl.when(relays[side])
                    def _(h=h, q=q, side=side):
                        onward(h, side, q).wait_send()

            for copy in outputs(h, q):
                copy.wait()


def local(
    conserved,
    register,
    stream_blocks,
    wall_matrix,
    span_blocks,
    inflow_gain,
    source_block,
    source_column,
):
    shape = (5, 8, 4, 32, 256)
    anywhere = pl.BlockSpec(memory_space=pl.ANY)
    vmem = pl.BlockSpec(memory_space=pltpu.VMEM)
    dma = pltpu.SemaphoreType.DMA
    halved = (2, 5, 8, 4, 32, 128)
    new_conserved, new_register = pl.pallas_call(
        kernel,
        out_shape=[jax.ShapeDtypeStruct(shape, F32)] * 2,
        in_specs=[
            anywhere,
            anywhere,
            vmem,
            vmem,
            vmem,
            pl.BlockSpec(memory_space=pltpu.SMEM),
            vmem,
            vmem,
        ],
        out_specs=[anywhere, anywhere],
        scratch_shapes=[
            pltpu.VMEM(halved, F32),
            pltpu.VMEM((2, 4, 5, 8, 32, 128), F32),
            pltpu.VMEM((2, 4, 5, 8, 32, 128), F32),
            pltpu.VMEM(halved, F32),
            pltpu.VMEM(halved, F32),
            pltpu.VMEM((2,) + halved, F32),
            pltpu.VMEM((2, RELAYED, 5, 2, 4, 32, 128), F32),
            pltpu.VMEM((1536, 640), BF16),
            pltpu.VMEM((640, 512), BF16),
            pltpu.VMEM((256, 768), BF16),
            pltpu.VMEM((256, 768), BF16),
            pltpu.VMEM((256, 2304), BF16),
            pltpu.VMEM((128, 1024), F32),
            pltpu.VMEM((8, 16, 128), F32),
            pltpu.VMEM((16, 8, 128), F32),
            pltpu.VMEM((16, 8, 128), F32),
            dma((4,)),
            dma((2, 4, 8)),
            dma((2, 4, 8)),
            dma((2, 4, 8)),
            dma((2, 4, 8)),
            dma((2, 2, 4)),
            dma((2, 2, 4)),
            dma((2, RELAYED)),
            dma((2, RELAYED)),
            dma((8,)),
            dma((8,)),
            dma((16,)),
            dma((16,)),
            dma((2, 2, 4)),
        ],
        compiler_params=pltpu.CompilerParams(
            collective_id=0, has_side_effects=True, vmem_limit_bytes=60 * 2**20
        ),
        name="section",
    )(
        conserved.reshape(shape),
        register.reshape(shape),
        stream_blocks,
        wall_matrix,
        span_blocks,
        inflow_gain,
        source_block.reshape(128, 1024),
        source_column,
    )
    return new_conserved.reshape(conserved.shape), new_register.reshape(register.shape)


def solution(mesh):
    split = P(None, "pz", "py", None)
    return jax.shard_map(
        local,
        mesh=mesh,
        in_specs=(split, split, P(), P(), P(), P(), P(), P()),
        out_specs=(split, split),
        check_vma=False,
    )
```

```python
import functools

import jax
import jax.numpy as jnp
from jax import lax
from jax.experimental import pallas as pl
from jax.experimental.pallas import tpu as pltpu
from jax.sharding import PartitionSpec as P

MESH = pl.DeviceIdType.MESH
F32 = jnp.float32
BF16 = jnp.bfloat16
SECTION_DECAY = -5.0 / 9.0
SECTION_GAIN = 15.0 / 16.0
TIME_STEP = 0.1
ORDER = (4, 1, 3, 5, 7, 6, 2)
RELAYED = 2
VMEM_MIB = 50


def flux(direction, density, first, second, third, energy):
    inverse = 1.0 / density
    moments = (first, second, third)
    speeds = tuple(moment * inverse for moment in moments)
    pressure = 0.4 * (
        energy - 0.5 * (first * speeds[0] + second * speeds[1] + third * speeds[2])
    )
    velocity = speeds[direction]
    pieces = [moments[direction]]
    for component in range(3):
        moment = moments[component] * velocity
        if component == direction:
            moment = moment + pressure
        pieces.append(moment)
    pieces.append((energy + pressure) * velocity)
    return pieces


def halves(value):
    high = value.astype(BF16)
    return high, (value - high.astype(F32)).astype(BF16)


def thirds(value):
    high = value.astype(BF16)
    rest = value - high.astype(F32)
    middle = rest.astype(BF16)
    return high, middle, (rest - middle.astype(F32)).astype(BF16)


def mm(left, right):
    return jnp.dot(left, right, preferred_element_type=F32)


def iota(shape, axis):
    return lax.broadcasted_iota(jnp.int32, shape, axis)


def kernel(
    con,
    reg,
    stream_in,
    wall_in,
    span_in,
    gain,
    source_block,
    source_column,
    out_con,
    out_reg,
    cur,
    got,
    wall_out,
    back,
    halo,
    hop,
    work,
    stream_work,
    wall_w,
    stream_w,
    span_w,
    slot_key,
    picked,
    staged,
    received,
    load_sem,
    fs,
    fr,
    bs,
    br,
    hs,
    hr,
    ps,
    pr,
    s1s,
    s1r,
    s2s,
    s2r,
):
    py, pz = lax.axis_index("py"), lax.axis_index("pz")
    me = py * 16 + pz

    def peer(offset):
        return lax.rem(py // 4 + offset // 4, 2) * 4 + lax.rem(lax.rem(py, 4) + offset % 4, 4)

    def half(h):
        return pl.ds(128 * h, 128)

    def remote(src, dst, send, recv, device):
        return pltpu.make_async_remote_copy(
            src_ref=src,
            dst_ref=dst,
            send_sem=send,
            recv_sem=recv,
            device_id=device,
            device_id_type=MESH,
        )

    def forward(h, q, offset):
        p = peer(offset)
        src = con.at[:, p, q, :, half(1)] if h == 1 else cur.at[0, :, p, q]
        return remote(
            src, got.at[h, q, :, py], fs.at[h, q, offset], fr.at[h, q, offset], (p, pz)
        )

    def own(h, q):
        src = con.at[:, py, q, :, half(1)] if h == 1 else cur.at[0, :, py, q]
        return pltpu.make_async_copy(src, got.at[h, q, :, py], fr.at[h, q, 0])

    def giveback(h, q, offset):
        p = peer(offset)
        return remote(
            wall_out.at[h, q, :, p],
            back.at[h, :, py, q],
            bs.at[h, q, offset],
            br.at[h, q, offset],
            (p, pz),
        )

    def beside(h, side, i):
        rows = pl.ds(2 * i, 2)
        src = con.at[:, rows, :, :, half(1)] if h == 1 else cur.at[0, :, rows]
        target = lax.rem(pz + (1 if side == 0 else 15), 16)
        return remote(
            src, halo.at[side, h, :, rows], hs.at[h, side, i], hr.at[h, side, i], (py, target)
        )

    def passing(h, side, i):
        rows = pl.ds(2 * i, 2)
        src = con.at[:, rows, :, :, half(1)] if h == 1 else cur.at[0, :, rows]
        target = lax.rem(pz + (14 if side == 0 else 2), 16)
        return remote(src, hop.at[h, i], hs.at[h, side, i], pr.at[h, i], (py, target))

    def onward(h, side, i):
        target = lax.rem(pz + (3 if side == 0 else 13), 16)
        return remote(
            hop.at[h, i],
            halo.at[side, h, :, pl.ds(2 * i, 2)],
            ps.at[h, i],
            hr.at[h, side, i],
            (py, target),
        )

    wraps = [lax.rem(pz, 8) == 7, lax.rem(pz, 8) == 0]
    relays = [lax.rem(pz, 8) == 5, lax.rem(pz, 8) == 2]

    def send_onward(h, i):
        for side in range(2):

            @pl.when(relays[side])
            def _(side=side):
                passing(h, side, i).wait_recv()
                onward(h, side, i).start()

    def send_forward(h, q):
        own(h, q).start()
        for offset in ORDER:
            forward(h, q, offset).start()

    def send_beside(h, i):
        for side in range(2):
            if i < RELAYED:

                @pl.when(wraps[side])
                def _(side=side):
                    passing(h, side, i).start()

                @pl.when(jnp.logical_not(wraps[side]))
                def _(side=side):
                    beside(h, side, i).start()

            else:
                beside(h, side, i).start()

    def stage_one(offset):
        p = peer(offset)
        return remote(
            picked.at[p], staged.at[:, py], s1s.at[offset], s1r.at[offset], (p, pz)
        )

    def stage_two(offset):
        target = lax.rem(pz + offset, 16)
        return remote(
            staged.at[target], received.at[pz], s2s.at[offset], s2r.at[offset], (py, target)
        )

    loads = [
        pltpu.make_async_copy(con.at[:, :, :, :, half(h)], cur.at[h], load_sem.at[h])
        for h in (1, 0)
    ] + [pltpu.make_async_copy(reg, out_reg, load_sem.at[2])]
    for load in loads:
        load.start()

    barrier = pltpu.get_barrier_semaphore()
    for offset in range(1, 8):
        pl.semaphore_signal(barrier, inc=1, device_id=(peer(offset), pz), device_id_type=MESH)
    for offset in range(1, 16):
        pl.semaphore_signal(
            barrier, inc=1, device_id=(py, lax.rem(pz + offset, 16)), device_id_type=MESH
        )
    pl.semaphore_wait(barrier, 22)

    send_beside(1, 0)
    send_forward(1, 0)
    send_beside(1, 1)
    send_forward(1, 1)

    lane = iota((128, 128), 1)
    row = iota((128, 128), 0)
    strict = jnp.where(row < lane, 1.0, 0.0).astype(BF16)
    counts = jnp.concatenate([strict, jnp.ones((128, 128), BF16)], axis=1)
    passed = jnp.zeros((128, 128), F32)
    for g in range(8):
        mine = source_block[:, 0, 128 * g : 128 * g + 128] == me
        ranked = mm(jnp.where(mine, 1.0, 0.0).astype(BF16), counts)
        slot_key[:, 128 * g : 128 * g + 128] = jnp.where(mine, ranked[:, :128] + passed, -1.0)
        passed = passed + ranked[:, 128:]

    loads[0].wait()
    for g in range(8):
        plane = jnp.zeros((128, 128), F32)
        for f in range(5):
            value = cur[1, f, g].reshape(128, 128)
            plane = plane + jnp.where(
                lane == f, jnp.broadcast_to(value[:, 64:65], (128, 128)), 0.0
            )
        for part, piece in enumerate(thirds(plane)):
            work[pl.ds(128 * g, 128), 128 * part : 128 * part + 128] = piece

    def pick(r, carry):
        total = jnp.zeros((128, 128), F32)
        for g in range(8):
            columns = source_column[:, 128 * g : 128 * g + 128].astype(F32)
            total = total + jnp.where(
                slot_key[:, 128 * g : 128 * g + 128] == r.astype(F32), columns, 0.0
            )
        wanted = jnp.sum(total, axis=1, keepdims=True)
        choose = jnp.concatenate(
            [
                jnp.where((lane + 128 * g).astype(F32) == wanted, 1.0, 0.0).astype(BF16)
                for g in range(8)
            ],
            axis=1,
        )
        values = mm(choose, work[pl.ds(0, 1024), 0:384])
        values = values[:, :128] + values[:, 128:256] + values[:, 256:384]
        return carry + pltpu.roll(values, 8 * r, 1)

    picked[...] = lax.fori_loop(0, 16, pick, jnp.zeros((128, 128), F32)).reshape(8, 16, 128)

    for offset in range(1, 8):
        stage_one(offset).start()
    for p in range(8):

        @pl.when(py == p)
        def _(p=p):
            staged[:, p, :] = picked[p]

    send_onward(1, 0)
    send_forward(1, 2)
    send_beside(1, 2)

    high, low = halves(wall_in[...])
    wall_w[:, 0:256] = high
    wall_w[:, 256:512] = high
    wall_w[:, 512:768] = low
    for k in range(2):
        for j in range(2):
            high, low = halves(stream_in[k, j - k + 1])
            rows = slice(128 * k, 128 * k + 128)
            stream_w[rows, 128 * j : 128 * j + 128] = high
            stream_w[rows, 256 + 128 * j : 256 + 128 * j + 128] = high
            stream_w[rows, 512 + 128 * j : 512 + 128 * j + 128] = low
    spread = jnp.where(iota((256, 32), 0) // 8 == iota((256, 32), 1), 1.0, 0.0).astype(BF16)
    aligned = lax.rem(iota((256, 256), 0), 8) == lax.rem(iota((256, 256), 1), 8)
    for j in range(3):
        for part, piece in enumerate(halves(span_in[pz, j])):
            wide = mm(spread, piece).astype(BF16)
            full = lax.dot_general(
                wide, spread, (((1,), (1,)), ((), ())), preferred_element_type=F32
            )
            full = jnp.where(aligned, full, 0.0).astype(BF16)
            if part == 0:
                span_w[:, 256 * j : 256 * j + 256] = full
                span_w[:, 768 + 256 * j : 768 + 256 * j + 256] = full
            else:
                span_w[:, 1536 + 256 * j : 1536 + 256 * j + 256] = full

    for offset in range(1, 8):
        stage_one(offset).wait_recv()
    for offset in range(1, 16):
        stage_two(offset).start()
    for p in range(16):

        @pl.when(pz == p)
        def _(p=p):
            received[p] = staged[p]

    send_onward(1, 1)
    send_forward(1, 3)
    send_beside(1, 3)
    loads[1].wait()
    for offset in range(1, 16):
        stage_two(offset).wait_recv()

    arrived = jnp.concatenate(thirds(received[...].reshape(128, 128)), axis=1)
    below = jnp.where(lane < row, 1.0, 0.0).astype(BF16)
    before = jnp.zeros((1, 128), F32)
    sources = source_block[me]
    sources = ((sources & 15) * 8 + (sources >> 4)).astype(F32)
    for g in range(8):
        named = jnp.broadcast_to(sources[:, 128 * g : 128 * g + 128], (128, 128)).T
        flags = jnp.where(named == lane.astype(F32), 1.0, 0.0)
        ahead = mm(below, flags.astype(BF16)) + before
        before = before + jnp.sum(flags, axis=0, keepdims=True)
        rank = jnp.sum(flags * ahead, axis=1, keepdims=True)
        values = mm(flags.astype(BF16), arrived)
        values = values[:, :128] + values[:, 128:256] + values[:, 256:384]
        values = jnp.where((lane // 8).astype(F32) == rank, values, 0.0)
        for shift in (64, 32, 16, 8):
            values = values + pltpu.roll(values, shift, 1)
        for f in range(5):
            column = jnp.broadcast_to(values[:, f : f + 1] * gain[f], (128, 128))
            old = cur[0, f, g].reshape(128, 128)
            cur[0, f, g] = jnp.where(lane == 0, column, old).reshape(4, 32, 128)

    for q in range(4):
        send_beside(0, q)
        send_forward(0, q)

    loads[2].wait()

    def stream(p, carry):
        for q in range(4):
            for h in range(2):
                pieces = flux(0, *[cur[h, f, p, q] for f in range(5)])
                for f in range(5):
                    high, low = halves(pieces[f])
                    rows = pl.ds(128 * f + 32 * q, 32)
                    stream_work[rows, 128 * h : 128 * h + 128] = high
                    stream_work[rows, 256 + 128 * h : 384 + 128 * h] = low
        nt = (((1,), (1,)), ((), ()))
        term = lax.dot_general(
            stream_work[...], stream_w[:, 0:512], nt, preferred_element_type=F32
        ) + lax.dot_general(
            stream_work[:, 0:256], stream_w[:, 512:768], nt, preferred_element_type=F32
        )
        for f in range(5):
            for h in range(2):
                part = term[128 * f : 128 * f + 128, 128 * h : 128 * h + 128]
                old = out_reg[f, p, :, :, half(h)]
                out_reg[f, p, :, :, half(h)] = (
                    SECTION_DECAY * old - TIME_STEP * part.reshape(4, 32, 128)
                )
        return carry

    lax.fori_loop(0, 8, stream, 0)
    for i in range(RELAYED):
        send_onward(0, i)

    def wall(h, q):
        own(h, q).wait()
        for offset in range(1, 8):
            forward(h, q, offset).wait_recv()

        def fill(s, carry):
            pieces = flux(1, *[got[h, q, f, s] for f in range(5)])
            for f in range(5):
                high, low = halves(pieces[f])
                work[pl.ds(32 * s, 32), 128 * f : 128 * f + 128] = high
                work[pl.ds(256 + 32 * s, 32), 128 * f : 128 * f + 128] = low
            return carry

        lax.fori_loop(0, 8, fill, 0)
        term = mm(wall_w[:, 0:512], work[pl.ds(0, 512), :]) + mm(
            wall_w[:, 512:768], work[pl.ds(0, 256), :]
        )
        for f in range(5):
            wall_out[h, q, f] = term[:, 128 * f : 128 * f + 128].reshape(8, 32, 128)
        for offset in ORDER:
            giveback(h, q, offset).start()
        for f in range(5):
            back[h, f, py, q] = wall_out[h, q, f, py]

    def span(h):
        for side in range(2):
            for i in range(4):
                beside(h, side, i).wait_recv()

        def tile(t, carry):
            rows = pl.ds(pl.multiple_of(8 * t, 8), 8)

            def fill(p, inner):
                for j in range(3):
                    if j == 1:
                        fields = [cur[h, f, p, :, rows, :] for f in range(5)]
                    else:
                        fields = [halo[j // 2, h, f, p, :, rows, :] for f in range(5)]
                    pieces = flux(2, *[field.reshape(32, 128) for field in fields])
                    for f in range(5):
                        high, low = halves(pieces[f])
                        work[pl.ds(256 * j + 32 * p, 32), 128 * f : 128 * f + 128] = high
                        work[pl.ds(768 + 256 * j + 32 * p, 32), 128 * f : 128 * f + 128] = low
                return inner

            lax.fori_loop(0, 8, fill, 0)
            term = mm(span_w[:, 0:1536], work[...]) + mm(
                span_w[:, 1536:2304], work[pl.ds(0, 768), :]
            )
            for f in range(5):
                part = term[:, 128 * f : 128 * f + 128].reshape(8, 4, 8, 128)
                old = out_reg[f, :, :, rows, half(h)]
                out_reg[f, :, :, rows, half(h)] = old - TIME_STEP * part
            return carry

        lax.fori_loop(0, 4, tile, 0)

    def finish(h, q):
        for offset in range(1, 8):
            giveback(h, q, offset).wait_recv()

        def join(p, carry):
            for f in range(5):
                fresh = out_reg[f, p, q, :, half(h)] - TIME_STEP * back[h, f, p, q]
                out_reg[f, p, q, :, half(h)] = fresh
                out_con[f, p, q, :, half(h)] = cur[h, f, p, q] + SECTION_GAIN * fresh
            return carry

        lax.fori_loop(0, 8, join, 0)

    for q in range(4):
        wall(1, q)
    span(1)
    for q in range(4):
        wall(0, q)
    span(0)
    for h in (1, 0):
        for q in range(4):
            finish(h, q)

    for offset in range(1, 8):
        stage_one(offset).wait_send()
    for offset in range(1, 16):
        stage_two(offset).wait_send()
    for h in (1, 0):
        for q in range(4):
            for offset in range(1, 8):
                forward(h, q, offset).wait_send()
                giveback(h, q, offset).wait_send()
            for side in range(2):
                beside(h, side, q).wait_send()
                if q < RELAYED:

                    @pl.when(relays[side])
                    def _(h=h, q=q, side=side):
                        onward(h, side, q).wait_send()


def local(
    conserved,
    register,
    stream_blocks,
    wall_matrix,
    span_blocks,
    inflow_gain,
    source_block,
    source_column,
):
    shape = (5, 8, 4, 32, 256)
    anywhere = pl.BlockSpec(memory_space=pl.ANY)
    vmem = pl.BlockSpec(memory_space=pltpu.VMEM)
    dma = pltpu.SemaphoreType.DMA
    halved = (2, 5, 8, 4, 32, 128)
    new_conserved, new_register = pl.pallas_call(
        kernel,
        out_shape=[pltpu.VMEM(shape, F32)] * 2,
        in_specs=[
            anywhere,
            anywhere,
            vmem,
            vmem,
            vmem,
            pl.BlockSpec(memory_space=pltpu.SMEM),
            vmem,
            vmem,
        ],
        out_specs=[vmem, vmem],
        scratch_shapes=[
            pltpu.VMEM(halved, F32),
            pltpu.VMEM((2, 4, 5, 8, 32, 128), F32),
            pltpu.VMEM((2, 4, 5, 8, 32, 128), F32),
            pltpu.VMEM(halved, F32),
            pltpu.VMEM((2,) + halved, F32),
            pltpu.VMEM((2, RELAYED, 5, 2, 4, 32, 128), F32),
            pltpu.VMEM((1536, 640), BF16),
            pltpu.VMEM((640, 512), BF16),
            pltpu.VMEM((256, 768), BF16),
            pltpu.VMEM((256, 768), BF16),
            pltpu.VMEM((256, 2304), BF16),
            pltpu.VMEM((128, 1024), F32),
            pltpu.VMEM((8, 16, 128), F32),
            pltpu.VMEM((16, 8, 128), F32),
            pltpu.VMEM((16, 8, 128), F32),
            dma((4,)),
            dma((2, 4, 8)),
            dma((2, 4, 8)),
            dma((2, 4, 8)),
            dma((2, 4, 8)),
            dma((2, 2, 4)),
            dma((2, 2, 4)),
            dma((2, RELAYED)),
            dma((2, RELAYED)),
            dma((8,)),
            dma((8,)),
            dma((16,)),
            dma((16,)),
        ],
        compiler_params=pltpu.CompilerParams(
            collective_id=0, has_side_effects=True, vmem_limit_bytes=VMEM_MIB * 2**20
        ),
        name="section",
    )(
        conserved.reshape(shape),
        register.reshape(shape),
        stream_blocks,
        wall_matrix,
        span_blocks,
        inflow_gain,
        jnp.swapaxes(source_block, 1, 2),
        source_column,
    )
    return new_conserved.reshape(conserved.shape), new_register.reshape(register.shape)


def solution(mesh):
    split = P(None, "pz", "py", None)
    return jax.shard_map(
        local,
        mesh=mesh,
        in_specs=(split, split, P(), P(), P(), P(), P(), P()),
        out_specs=(split, split),
        check_vma=False,
    )
```

```python
import functools

import jax
import jax.numpy as jnp
from jax import lax
from jax.experimental import pallas as pl
from jax.experimental.pallas import tpu as pltpu
from jax.sharding import PartitionSpec as P

MESH = pl.DeviceIdType.MESH
F32 = jnp.float32
BF16 = jnp.bfloat16
SECTION_DECAY = -5.0 / 9.0
SECTION_GAIN = 15.0 / 16.0
TIME_STEP = 0.1
ORDER = (6, 2, 5, 7, 1, 3, 4)
RELAYED = 2
VMEM_MIB = 50


def flux(direction, density, first, second, third, energy):
    inverse = 1.0 / density
    moments = (first, second, third)
    speeds = tuple(moment * inverse for moment in moments)
    pressure = 0.4 * (
        energy - 0.5 * (first * speeds[0] + second * speeds[1] + third * speeds[2])
    )
    velocity = speeds[direction]
    pieces = [moments[direction]]
    for component in range(3):
        moment = moments[component] * velocity
        if component == direction:
            moment = moment + pressure
        pieces.append(moment)
    pieces.append((energy + pressure) * velocity)
    return pieces


def halves(value):
    high = value.astype(BF16)
    return high, (value - high.astype(F32)).astype(BF16)


def thirds(value):
    high = value.astype(BF16)
    rest = value - high.astype(F32)
    middle = rest.astype(BF16)
    return high, middle, (rest - middle.astype(F32)).astype(BF16)


def mm(left, right):
    return jnp.dot(left, right, preferred_element_type=F32)


def iota(shape, axis):
    return lax.broadcasted_iota(jnp.int32, shape, axis)


def kernel(
    con,
    reg,
    stream_in,
    wall_in,
    span_in,
    gain,
    source_block,
    source_column,
    out_con,
    out_reg,
    cur,
    got,
    wall_out,
    back,
    halo,
    hop,
    work,
    stream_work,
    wall_w,
    stream_w,
    span_w,
    slot_key,
    picked,
    staged,
    received,
    load_sem,
    fs,
    fr,
    bs,
    br,
    hs,
    hr,
    ps,
    pr,
    s1s,
    s1r,
    s2s,
    s2r,
):
    py, pz = lax.axis_index("py"), lax.axis_index("pz")
    me = py * 16 + pz

    def peer(offset):
        return lax.rem(py // 4 + offset // 4, 2) * 4 + lax.rem(lax.rem(py, 4) + offset % 4, 4)

    def half(h):
        return pl.ds(128 * h, 128)

    def remote(src, dst, send, recv, device):
        return pltpu.make_async_remote_copy(
            src_ref=src,
            dst_ref=dst,
            send_sem=send,
            recv_sem=recv,
            device_id=device,
            device_id_type=MESH,
        )

    def forward(h, q, offset):
        p = peer(offset)
        src = con.at[:, p, q, :, half(1)] if h == 1 else cur.at[0, :, p, q]
        return remote(
            src, got.at[h, q, :, py], fs.at[h, q, offset], fr.at[h, q, offset], (p, pz)
        )

    def own(h, q):
        src = con.at[:, py, q, :, half(1)] if h == 1 else cur.at[0, :, py, q]
        return pltpu.make_async_copy(src, got.at[h, q, :, py], fr.at[h, q, 0])

    def giveback(h, q, offset):
        p = peer(offset)
        return remote(
            wall_out.at[h, q, :, p],
            back.at[h, :, py, q],
            bs.at[h, q, offset],
            br.at[h, q, offset],
            (p, pz),
        )

    def beside(h, side, i):
        rows = pl.ds(2 * i, 2)
        src = con.at[:, rows, :, :, half(1)] if h == 1 else cur.at[0, :, rows]
        target = lax.rem(pz + (1 if side == 0 else 15), 16)
        return remote(
            src, halo.at[side, h, :, rows], hs.at[h, side, i], hr.at[h, side, i], (py, target)
        )

    def passing(h, side, i):
        rows = pl.ds(2 * i, 2)
        src = con.at[:, rows, :, :, half(1)] if h == 1 else cur.at[0, :, rows]
        target = lax.rem(pz + (14 if side == 0 else 2), 16)
        return remote(src, hop.at[h, i], hs.at[h, side, i], pr.at[h, i], (py, target))

    def onward(h, side, i):
        target = lax.rem(pz + (3 if side == 0 else 13), 16)
        return remote(
            hop.at[h, i],
            halo.at[side, h, :, pl.ds(2 * i, 2)],
            ps.at[h, i],
            hr.at[h, side, i],
            (py, target),
        )

    wraps = [lax.rem(pz, 8) == 7, lax.rem(pz, 8) == 0]
    relays = [lax.rem(pz, 8) == 5, lax.rem(pz, 8) == 2]

    def send_onward(h, i):
        for side in range(2):

            @pl.when(relays[side])
            def _(side=side):
                passing(h, side, i).wait_recv()
                onward(h, side, i).start()

    def send_forward(h, q):
        own(h, q).start()
        for offset in ORDER:
            forward(h, q, offset).start()

    def send_beside(h, i):
        for side in range(2):
            if i < RELAYED:

                @pl.when(wraps[side])
                def _(side=side):
                    passing(h, side, i).start()

                @pl.when(jnp.logical_not(wraps[side]))
                def _(side=side):
                    beside(h, side, i).start()

            else:
                beside(h, side, i).start()

    def stage_one(offset):
        p = peer(offset)
        return remote(
            picked.at[p], staged.at[:, py], s1s.at[offset], s1r.at[offset], (p, pz)
        )

    def stage_two(offset):
        target = lax.rem(pz + offset, 16)
        return remote(
            staged.at[target], received.at[pz], s2s.at[offset], s2r.at[offset], (py, target)
        )

    loads = [
        pltpu.make_async_copy(con.at[:, :, :, :, half(h)], cur.at[h], load_sem.at[h])
        for h in (1, 0)
    ] + [pltpu.make_async_copy(reg, out_reg, load_sem.at[2])]
    for load in loads:
        load.start()

    barrier = pltpu.get_barrier_semaphore()
    for offset in range(1, 8):
        pl.semaphore_signal(barrier, inc=1, device_id=(peer(offset), pz), device_id_type=MESH)
    for offset in range(1, 16):
        pl.semaphore_signal(
            barrier, inc=1, device_id=(py, lax.rem(pz + offset, 16)), device_id_type=MESH
        )
    pl.semaphore_wait(barrier, 22)

    send_beside(1, 0)
    send_forward(1, 0)
    send_beside(1, 1)
    send_forward(1, 1)

    lane = iota((128, 128), 1)
    row = iota((128, 128), 0)
    strict = jnp.where(row < lane, 1.0, 0.0).astype(BF16)
    counts = jnp.concatenate([strict, jnp.ones((128, 128), BF16)], axis=1)
    passed = jnp.zeros((128, 128), F32)
    for g in range(8):
        mine = source_block[:, 0, 128 * g : 128 * g + 128] == me
        ranked = mm(jnp.where(mine, 1.0, 0.0).astype(BF16), counts)
        slot_key[:, 128 * g : 128 * g + 128] = jnp.where(mine, ranked[:, :128] + passed, -1.0)
        passed = passed + ranked[:, 128:]

    loads[0].wait()
    for g in range(8):
        plane = jnp.zeros((128, 128), F32)
        for f in range(5):
            value = cur[1, f, g].reshape(128, 128)
            plane = plane + jnp.where(
                lane == f, jnp.broadcast_to(value[:, 64:65], (128, 128)), 0.0
            )
        for part, piece in enumerate(thirds(plane)):
            work[pl.ds(128 * g, 128), 128 * part : 128 * part + 128] = piece

    def pick(r, carry):
        total = jnp.zeros((128, 128), F32)
        for g in range(8):
            columns = source_column[:, 128 * g : 128 * g + 128].astype(F32)
            total = total + jnp.where(
                slot_key[:, 128 * g : 128 * g + 128] == r.astype(F32), columns, 0.0
            )
        wanted = jnp.sum(total, axis=1, keepdims=True)
        choose = jnp.concatenate(
            [
                jnp.where((lane + 128 * g).astype(F32) == wanted, 1.0, 0.0).astype(BF16)
                for g in range(8)
            ],
            axis=1,
        )
        values = mm(choose, work[pl.ds(0, 1024), 0:384])
        values = values[:, :128] + values[:, 128:256] + values[:, 256:384]
        return carry + pltpu.roll(values, 8 * r, 1)

    picked[...] = lax.fori_loop(0, 16, pick, jnp.zeros((128, 128), F32)).reshape(8, 16, 128)

    for offset in range(1, 8):
        stage_one(offset).start()
    for p in range(8):

        @pl.when(py == p)
        def _(p=p):
            staged[:, p, :] = picked[p]

    send_onward(1, 0)
    send_forward(1, 2)
    send_beside(1, 2)

    high, low = halves(wall_in[...])
    wall_w[:, 0:256] = high
    wall_w[:, 256:512] = high
    wall_w[:, 512:768] = low
    for k in range(2):
        for j in range(2):
            high, low = halves(stream_in[k, j - k + 1])
            rows = slice(128 * k, 128 * k + 128)
            stream_w[rows, 128 * j : 128 * j + 128] = high
            stream_w[rows, 256 + 128 * j : 256 + 128 * j + 128] = high
            stream_w[rows, 512 + 128 * j : 512 + 128 * j + 128] = low
    spread = jnp.where(iota((256, 32), 0) // 8 == iota((256, 32), 1), 1.0, 0.0).astype(BF16)
    aligned = lax.rem(iota((256, 256), 0), 8) == lax.rem(iota((256, 256), 1), 8)
    for j in range(3):
        for part, piece in enumerate(halves(span_in[pz, j])):
            wide = mm(spread, piece).astype(BF16)
            full = lax.dot_general(
                wide, spread, (((1,), (1,)), ((), ())), preferred_element_type=F32
            )
            full = jnp.where(aligned, full, 0.0).astype(BF16)
            if part == 0:
                span_w[:, 256 * j : 256 * j + 256] = full
                span_w[:, 768 + 256 * j : 768 + 256 * j + 256] = full
            else:
                span_w[:, 1536 + 256 * j : 1536 + 256 * j + 256] = full

    for offset in range(1, 8):
        stage_one(offset).wait_recv()
    for offset in range(1, 16):
        stage_two(offset).start()
    for p in range(16):

        @pl.when(pz == p)
        def _(p=p):
            received[p] = staged[p]

    send_onward(1, 1)
    send_forward(1, 3)
    send_beside(1, 3)
    loads[1].wait()
    for offset in range(1, 16):
        stage_two(offset).wait_recv()

    arrived = jnp.concatenate(thirds(received[...].reshape(128, 128)), axis=1)
    below = jnp.where(lane < row, 1.0, 0.0).astype(BF16)
    before = jnp.zeros((1, 128), F32)
    sources = source_block[me]
    sources = ((sources & 15) * 8 + (sources >> 4)).astype(F32)
    for g in range(8):
        named = jnp.broadcast_to(sources[:, 128 * g : 128 * g + 128], (128, 128)).T
        flags = jnp.where(named == lane.astype(F32), 1.0, 0.0)
        ahead = mm(below, flags.astype(BF16)) + before
        before = before + jnp.sum(flags, axis=0, keepdims=True)
        rank = jnp.sum(flags * ahead, axis=1, keepdims=True)
        values = mm(flags.astype(BF16), arrived)
        values = values[:, :128] + values[:, 128:256] + values[:, 256:384]
        values = jnp.where((lane // 8).astype(F32) == rank, values, 0.0)
        for shift in (64, 32, 16, 8):
            values = values + pltpu.roll(values, shift, 1)
        for f in range(5):
            column = jnp.broadcast_to(values[:, f : f + 1] * gain[f], (128, 128))
            old = cur[0, f, g].reshape(128, 128)
            cur[0, f, g] = jnp.where(lane == 0, column, old).reshape(4, 32, 128)

    for q in range(4):
        send_beside(0, q)
        send_forward(0, q)

    loads[2].wait()

    def stream(p, carry):
        for q in range(4):
            for h in range(2):
                pieces = flux(0, *[cur[h, f, p, q] for f in range(5)])
                for f in range(5):
                    high, low = halves(pieces[f])
                    rows = pl.ds(128 * f + 32 * q, 32)
                    stream_work[rows, 128 * h : 128 * h + 128] = high
                    stream_work[rows, 256 + 128 * h : 384 + 128 * h] = low
        nt = (((1,), (1,)), ((), ()))
        term = lax.dot_general(
            stream_work[...], stream_w[:, 0:512], nt, preferred_element_type=F32
        ) + lax.dot_general(
            stream_work[:, 0:256], stream_w[:, 512:768], nt, preferred_element_type=F32
        )
        for f in range(5):
            for h in range(2):
                part = term[128 * f : 128 * f + 128, 128 * h : 128 * h + 128]
                old = out_reg[f, p, :, :, half(h)]
                out_reg[f, p, :, :, half(h)] = (
                    SECTION_DECAY * old - TIME_STEP * part.reshape(4, 32, 128)
                )
        return carry

    lax.fori_loop(0, 8, stream, 0)
    for i in range(RELAYED):
        send_onward(0, i)

    def wall(h, q):
        own(h, q).wait()
        for offset in range(1, 8):
            forward(h, q, offset).wait_recv()

        def fill(s, carry):
            pieces = flux(1, *[got[h, q, f, s] for f in range(5)])
            for f in range(5):
                high, low = halves(pieces[f])
                work[pl.ds(32 * s, 32), 128 * f : 128 * f + 128] = high
                work[pl.ds(256 + 32 * s, 32), 128 * f : 128 * f + 128] = low
            return carry

        lax.fori_loop(0, 8, fill, 0)
        term = mm(wall_w[:, 0:512], work[pl.ds(0, 512), :]) + mm(
            wall_w[:, 512:768], work[pl.ds(0, 256), :]
        )
        for f in range(5):
            wall_out[h, q, f] = term[:, 128 * f : 128 * f + 128].reshape(8, 32, 128)
        for offset in ORDER:
            giveback(h, q, offset).start()
        for f in range(5):
            back[h, f, py, q] = wall_out[h, q, f, py]

    def span(h):
        for side in range(2):
            for i in range(4):
                beside(h, side, i).wait_recv()

        def tile(t, carry):
            rows = pl.ds(pl.multiple_of(8 * t, 8), 8)

            def fill(p, inner):
                for j in range(3):
                    if j == 1:
                        fields = [cur[h, f, p, :, rows, :] for f in range(5)]
                    else:
                        fields = [halo[j // 2, h, f, p, :, rows, :] for f in range(5)]
                    pieces = flux(2, *[field.reshape(32, 128) for field in fields])
                    for f in range(5):
                        high, low = halves(pieces[f])
                        work[pl.ds(256 * j + 32 * p, 32), 128 * f : 128 * f + 128] = high
                        work[pl.ds(768 + 256 * j + 32 * p, 32), 128 * f : 128 * f + 128] = low
                return inner

            lax.fori_loop(0, 8, fill, 0)
            term = mm(span_w[:, 0:1536], work[...]) + mm(
                span_w[:, 1536:2304], work[pl.ds(0, 768), :]
            )
            for f in range(5):
                part = term[:, 128 * f : 128 * f + 128].reshape(8, 4, 8, 128)
                old = out_reg[f, :, :, rows, half(h)]
                out_reg[f, :, :, rows, half(h)] = old - TIME_STEP * part
            return carry

        lax.fori_loop(0, 4, tile, 0)

    def finish(h, q):
        for offset in range(1, 8):
            giveback(h, q, offset).wait_recv()

        def join(p, carry):
            for f in range(5):
                fresh = out_reg[f, p, q, :, half(h)] - TIME_STEP * back[h, f, p, q]
                out_reg[f, p, q, :, half(h)] = fresh
                out_con[f, p, q, :, half(h)] = cur[h, f, p, q] + SECTION_GAIN * fresh
            return carry

        lax.fori_loop(0, 8, join, 0)

    for q in range(4):
        wall(1, q)
    for q in range(4):
        wall(0, q)
    span(1)
    span(0)
    for h in (1, 0):
        for q in range(4):
            finish(h, q)

    for offset in range(1, 8):
        stage_one(offset).wait_send()
    for offset in range(1, 16):
        stage_two(offset).wait_send()
    for h in (1, 0):
        for q in range(4):
            for offset in range(1, 8):
                forward(h, q, offset).wait_send()
                giveback(h, q, offset).wait_send()
            for side in range(2):
                beside(h, side, q).wait_send()
                if q < RELAYED:

                    @pl.when(relays[side])
                    def _(h=h, q=q, side=side):
                        onward(h, side, q).wait_send()


def local(
    conserved,
    register,
    stream_blocks,
    wall_matrix,
    span_blocks,
    inflow_gain,
    source_block,
    source_column,
):
    shape = (5, 8, 4, 32, 256)
    anywhere = pl.BlockSpec(memory_space=pl.ANY)
    vmem = pl.BlockSpec(memory_space=pltpu.VMEM)
    dma = pltpu.SemaphoreType.DMA
    halved = (2, 5, 8, 4, 32, 128)
    new_conserved, new_register = pl.pallas_call(
        kernel,
        out_shape=[pltpu.VMEM(shape, F32)] * 2,
        in_specs=[
            anywhere,
            anywhere,
            vmem,
            vmem,
            vmem,
            pl.BlockSpec(memory_space=pltpu.SMEM),
            vmem,
            vmem,
        ],
        out_specs=[vmem, vmem],
        scratch_shapes=[
            pltpu.VMEM(halved, F32),
            pltpu.VMEM((2, 4, 5, 8, 32, 128), F32),
            pltpu.VMEM((2, 4, 5, 8, 32, 128), F32),
            pltpu.VMEM(halved, F32),
            pltpu.VMEM((2,) + halved, F32),
            pltpu.VMEM((2, RELAYED, 5, 2, 4, 32, 128), F32),
            pltpu.VMEM((1536, 640), BF16),
            pltpu.VMEM((640, 512), BF16),
            pltpu.VMEM((256, 768), BF16),
            pltpu.VMEM((256, 768), BF16),
            pltpu.VMEM((256, 2304), BF16),
            pltpu.VMEM((128, 1024), F32),
            pltpu.VMEM((8, 16, 128), F32),
            pltpu.VMEM((16, 8, 128), F32),
            pltpu.VMEM((16, 8, 128), F32),
            dma((4,)),
            dma((2, 4, 8)),
            dma((2, 4, 8)),
            dma((2, 4, 8)),
            dma((2, 4, 8)),
            dma((2, 2, 4)),
            dma((2, 2, 4)),
            dma((2, RELAYED)),
            dma((2, RELAYED)),
            dma((8,)),
            dma((8,)),
            dma((16,)),
            dma((16,)),
        ],
        compiler_params=pltpu.CompilerParams(
            collective_id=0, has_side_effects=True, vmem_limit_bytes=VMEM_MIB * 2**20
        ),
        name="section",
    )(
        conserved.reshape(shape),
        register.reshape(shape),
        stream_blocks,
        wall_matrix,
        span_blocks,
        inflow_gain,
        jnp.swapaxes(source_block, 1, 2),
        source_column,
    )
    return new_conserved.reshape(conserved.shape), new_register.reshape(register.shape)


def solution(mesh):
    split = P(None, "pz", "py", None)
    return jax.shard_map(
        local,
        mesh=mesh,
        in_specs=(split, split, P(), P(), P(), P(), P(), P()),
        out_specs=(split, split),
        check_vma=False,
    )
```

```python
import functools

import jax
import jax.numpy as jnp
from jax import lax
from jax.experimental import pallas as pl
from jax.experimental.pallas import tpu as pltpu
from jax.sharding import PartitionSpec as P

MESH = pl.DeviceIdType.MESH
F32 = jnp.float32
BF16 = jnp.bfloat16
SECTION_DECAY = -5.0 / 9.0
SECTION_GAIN = 15.0 / 16.0
TIME_STEP = 0.1
ORDER = (6, 2, 5, 7, 1, 3, 4)
RELAYED = 2
VMEM_MIB = 50


def flux(direction, density, first, second, third, energy):
    inverse = 1.0 / density
    moments = (first, second, third)
    speeds = tuple(moment * inverse for moment in moments)
    pressure = 0.4 * (
        energy - 0.5 * (first * speeds[0] + second * speeds[1] + third * speeds[2])
    )
    velocity = speeds[direction]
    pieces = [moments[direction]]
    for component in range(3):
        moment = moments[component] * velocity
        if component == direction:
            moment = moment + pressure
        pieces.append(moment)
    pieces.append((energy + pressure) * velocity)
    return pieces


def halves(value):
    high = value.astype(BF16)
    return high, (value - high.astype(F32)).astype(BF16)


def thirds(value):
    high = value.astype(BF16)
    rest = value - high.astype(F32)
    middle = rest.astype(BF16)
    return high, middle, (rest - middle.astype(F32)).astype(BF16)


def mm(left, right):
    return jnp.dot(left, right, preferred_element_type=F32)


def iota(shape, axis):
    return lax.broadcasted_iota(jnp.int32, shape, axis)


def kernel(
    con,
    reg,
    stream_in,
    wall_in,
    span_in,
    gain,
    source_block,
    source_column,
    out_con,
    out_reg,
    cur,
    got,
    wall_out,
    back,
    halo,
    hop,
    work,
    stream_work,
    wall_w,
    stream_w,
    span_w,
    slot_key,
    picked,
    staged,
    received,
    load_sem,
    fs,
    fr,
    bs,
    br,
    hs,
    hr,
    ps,
    pr,
    s1s,
    s1r,
    s2s,
    s2r,
):
    py, pz = lax.axis_index("py"), lax.axis_index("pz")
    me = py * 16 + pz

    def peer(offset):
        return lax.rem(py // 4 + offset // 4, 2) * 4 + lax.rem(lax.rem(py, 4) + offset % 4, 4)

    def half(h):
        return pl.ds(128 * h, 128)

    def remote(src, dst, send, recv, device):
        return pltpu.make_async_remote_copy(
            src_ref=src,
            dst_ref=dst,
            send_sem=send,
            recv_sem=recv,
            device_id=device,
            device_id_type=MESH,
        )

    def forward(h, q, offset):
        p = peer(offset)
        src = con.at[:, p, q, :, half(1)] if h == 1 else cur.at[0, :, p, q]
        return remote(
            src, got.at[h, q, :, py], fs.at[h, q, offset], fr.at[h, q, offset], (p, pz)
        )

    def own(h, q):
        src = con.at[:, py, q, :, half(1)] if h == 1 else cur.at[0, :, py, q]
        return pltpu.make_async_copy(src, got.at[h, q, :, py], fr.at[h, q, 0])

    def giveback(h, q, offset):
        p = peer(offset)
        return remote(
            wall_out.at[h, q, :, p],
            back.at[h, :, py, q],
            bs.at[h, q, offset],
            br.at[h, q, offset],
            (p, pz),
        )

    def beside(h, side, i):
        rows = pl.ds(2 * i, 2)
        src = con.at[:, rows, :, :, half(1)] if h == 1 else cur.at[0, :, rows]
        target = lax.rem(pz + (1 if side == 0 else 15), 16)
        return remote(
            src, halo.at[side, h, :, rows], hs.at[h, side, i], hr.at[h, side, i], (py, target)
        )

    def passing(h, side, i):
        rows = pl.ds(2 * i, 2)
        src = con.at[:, rows, :, :, half(1)] if h == 1 else cur.at[0, :, rows]
        target = lax.rem(pz + (14 if side == 0 else 2), 16)
        return remote(src, hop.at[h, i], hs.at[h, side, i], pr.at[h, i], (py, target))

    def onward(h, side, i):
        target = lax.rem(pz + (3 if side == 0 else 13), 16)
        return remote(
            hop.at[h, i],
            halo.at[side, h, :, pl.ds(2 * i, 2)],
            ps.at[h, i],
            hr.at[h, side, i],
            (py, target),
        )

    wraps = [lax.rem(pz, 8) == 7, lax.rem(pz, 8) == 0]
    relays = [lax.rem(pz, 8) == 5, lax.rem(pz, 8) == 2]

    def send_onward(h, i):
        for side in range(2):

            @pl.when(relays[side])
            def _(side=side):
                passing(h, side, i).wait_recv()
                onward(h, side, i).start()

    def send_forward(h, q):
        own(h, q).start()
        for offset in ORDER:
            forward(h, q, offset).start()

    def send_beside(h, i):
        for side in range(2):
            if i < RELAYED:

                @pl.when(wraps[side])
                def _(side=side):
                    passing(h, side, i).start()

                @pl.when(jnp.logical_not(wraps[side]))
                def _(side=side):
                    beside(h, side, i).start()

            else:
                beside(h, side, i).start()

    def stage_one(offset):
        p = peer(offset)
        return remote(
            picked.at[p], staged.at[:, py], s1s.at[offset], s1r.at[offset], (p, pz)
        )

    def stage_two(offset):
        target = lax.rem(pz + offset, 16)
        return remote(
            staged.at[target], received.at[pz], s2s.at[offset], s2r.at[offset], (py, target)
        )

    loads = [
        pltpu.make_async_copy(con.at[:, :, :, :, half(h)], cur.at[h], load_sem.at[h])
        for h in (1, 0)
    ] + [pltpu.make_async_copy(reg, out_reg, load_sem.at[2])]
    for load in loads:
        load.start()

    barrier = pltpu.get_barrier_semaphore()
    for offset in range(1, 8):
        pl.semaphore_signal(barrier, inc=1, device_id=(peer(offset), pz), device_id_type=MESH)
    for offset in range(1, 16):
        pl.semaphore_signal(
            barrier, inc=1, device_id=(py, lax.rem(pz + offset, 16)), device_id_type=MESH
        )
    pl.semaphore_wait(barrier, 22)

    send_beside(1, 0)
    send_forward(1, 0)
    send_beside(1, 1)
    send_forward(1, 1)

    lane = iota((128, 128), 1)
    row = iota((128, 128), 0)
    strict = jnp.where(row < lane, 1.0, 0.0).astype(BF16)
    counts = jnp.concatenate([strict, jnp.ones((128, 128), BF16)], axis=1)
    passed = jnp.zeros((128, 128), F32)
    for g in range(8):
        mine = source_block[:, 0, 128 * g : 128 * g + 128] == me
        ranked = mm(jnp.where(mine, 1.0, 0.0).astype(BF16), counts)
        slot_key[:, 128 * g : 128 * g + 128] = jnp.where(mine, ranked[:, :128] + passed, -1.0)
        passed = passed + ranked[:, 128:]

    loads[0].wait()
    for g in range(8):
        plane = jnp.zeros((128, 128), F32)
        for f in range(5):
            value = cur[1, f, g].reshape(128, 128)
            plane = plane + jnp.where(
                lane == f, jnp.broadcast_to(value[:, 64:65], (128, 128)), 0.0
            )
        for part, piece in enumerate(thirds(plane)):
            work[pl.ds(128 * g, 128), 128 * part : 128 * part + 128] = piece

    def pick(r, carry):
        total = jnp.zeros((128, 128), F32)
        for g in range(8):
            columns = source_column[:, 128 * g : 128 * g + 128].astype(F32)
            total = total + jnp.where(
                slot_key[:, 128 * g : 128 * g + 128] == r.astype(F32), columns, 0.0
            )
        wanted = jnp.sum(total, axis=1, keepdims=True)
        choose = jnp.concatenate(
            [
                jnp.where((lane + 128 * g).astype(F32) == wanted, 1.0, 0.0).astype(BF16)
                for g in range(8)
            ],
            axis=1,
        )
        values = mm(choose, work[pl.ds(0, 1024), 0:384])
        values = values[:, :128] + values[:, 128:256] + values[:, 256:384]
        return carry + pltpu.roll(values, 8 * r, 1)

    picked[...] = lax.fori_loop(0, 16, pick, jnp.zeros((128, 128), F32)).reshape(8, 16, 128)

    for offset in range(1, 8):
        stage_one(offset).start()
    for p in range(8):

        @pl.when(py == p)
        def _(p=p):
            staged[:, p, :] = picked[p]

    send_onward(1, 0)
    send_forward(1, 2)
    send_beside(1, 2)

    high, low = halves(wall_in[...])
    wall_w[:, 0:256] = high
    wall_w[:, 256:512] = high
    wall_w[:, 512:768] = low
    for k in range(2):
        for j in range(2):
            high, low = halves(stream_in[k, j - k + 1])
            rows = slice(128 * k, 128 * k + 128)
            stream_w[rows, 128 * j : 128 * j + 128] = high
            stream_w[rows, 256 + 128 * j : 256 + 128 * j + 128] = high
            stream_w[rows, 512 + 128 * j : 512 + 128 * j + 128] = low
    spread = jnp.where(iota((256, 32), 0) // 8 == iota((256, 32), 1), 1.0, 0.0).astype(BF16)
    aligned = lax.rem(iota((256, 256), 0), 8) == lax.rem(iota((256, 256), 1), 8)
    for j in range(3):
        for part, piece in enumerate(halves(span_in[pz, j])):
            wide = mm(spread, piece).astype(BF16)
            full = lax.dot_general(
                wide, spread, (((1,), (1,)), ((), ())), preferred_element_type=F32
            )
            full = jnp.where(aligned, full, 0.0).astype(BF16)
            if part == 0:
                span_w[:, 256 * j : 256 * j + 256] = full
                span_w[:, 768 + 256 * j : 768 + 256 * j + 256] = full
            else:
                span_w[:, 1536 + 256 * j : 1536 + 256 * j + 256] = full

    for offset in range(1, 8):
        stage_one(offset).wait_recv()
    for offset in range(1, 16):
        stage_two(offset).start()
    for p in range(16):

        @pl.when(pz == p)
        def _(p=p):
            received[p] = staged[p]

    send_onward(1, 1)
    send_forward(1, 3)
    send_beside(1, 3)
    loads[1].wait()
    for offset in range(1, 16):
        stage_two(offset).wait_recv()

    arrived = jnp.concatenate(thirds(received[...].reshape(128, 128)), axis=1)
    below = jnp.where(lane < row, 1.0, 0.0).astype(BF16)
    before = jnp.zeros((1, 128), F32)
    sources = source_block[me]
    sources = ((sources & 15) * 8 + (sources >> 4)).astype(F32)
    for g in range(8):
        named = jnp.broadcast_to(sources[:, 128 * g : 128 * g + 128], (128, 128)).T
        flags = jnp.where(named == lane.astype(F32), 1.0, 0.0)
        ahead = mm(below, flags.astype(BF16)) + before
        before = before + jnp.sum(flags, axis=0, keepdims=True)
        rank = jnp.sum(flags * ahead, axis=1, keepdims=True)
        values = mm(flags.astype(BF16), arrived)
        values = values[:, :128] + values[:, 128:256] + values[:, 256:384]
        values = jnp.where((lane // 8).astype(F32) == rank, values, 0.0)
        for shift in (64, 32, 16, 8):
            values = values + pltpu.roll(values, shift, 1)
        for f in range(5):
            column = jnp.broadcast_to(values[:, f : f + 1] * gain[f], (128, 128))
            old = cur[0, f, g].reshape(128, 128)
            cur[0, f, g] = jnp.where(lane == 0, column, old).reshape(4, 32, 128)

    for q in range(4):
        send_beside(0, q)
        send_forward(0, q)

    loads[2].wait()

    def stream(p, carry):
        for q in range(4):
            for h in range(2):
                pieces = flux(0, *[cur[h, f, p, q] for f in range(5)])
                for f in range(5):
                    high, low = halves(pieces[f])
                    rows = pl.ds(128 * f + 32 * q, 32)
                    stream_work[rows, 128 * h : 128 * h + 128] = high
                    stream_work[rows, 256 + 128 * h : 384 + 128 * h] = low
        nt = (((1,), (1,)), ((), ()))
        term = lax.dot_general(
            stream_work[...], stream_w[:, 0:512], nt, preferred_element_type=F32
        ) + lax.dot_general(
            stream_work[:, 0:256], stream_w[:, 512:768], nt, preferred_element_type=F32
        )
        for f in range(5):
            for h in range(2):
                part = term[128 * f : 128 * f + 128, 128 * h : 128 * h + 128]
                old = out_reg[f, p, :, :, half(h)]
                out_reg[f, p, :, :, half(h)] = (
                    SECTION_DECAY * old - TIME_STEP * part.reshape(4, 32, 128)
                )
        return carry

    lax.fori_loop(0, 8, stream, 0)
    for i in range(RELAYED):
        send_onward(0, i)

    def wall(h, q):
        own(h, q).wait()
        for offset in range(1, 8):
            forward(h, q, offset).wait_recv()

        def fill(s, carry):
            pieces = flux(1, *[got[h, q, f, s] for f in range(5)])
            for f in range(5):
                high, low = halves(pieces[f])
                work[pl.ds(32 * s, 32), 128 * f : 128 * f + 128] = high
                work[pl.ds(256 + 32 * s, 32), 128 * f : 128 * f + 128] = low
            return carry

        lax.fori_loop(0, 8, fill, 0)
        term = mm(wall_w[:, 0:512], work[pl.ds(0, 512), :]) + mm(
            wall_w[:, 512:768], work[pl.ds(0, 256), :]
        )
        for f in range(5):
            wall_out[h, q, f] = term[:, 128 * f : 128 * f + 128].reshape(8, 32, 128)
        for offset in ORDER:
            giveback(h, q, offset).start()
        for f in range(5):
            back[h, f, py, q] = wall_out[h, q, f, py]

    def span(h):
        for side in range(2):
            for i in range(4):
                beside(h, side, i).wait_recv()

        def tile(t, carry):
            rows = pl.ds(pl.multiple_of(8 * t, 8), 8)

            def fill(p, inner):
                for j in range(3):
                    if j == 1:
                        fields = [cur[h, f, p, :, rows, :] for f in range(5)]
                    else:
                        fields = [halo[j // 2, h, f, p, :, rows, :] for f in range(5)]
                    pieces = flux(2, *[field.reshape(32, 128) for field in fields])
                    for f in range(5):
                        high, low = halves(pieces[f])
                        work[pl.ds(256 * j + 32 * p, 32), 128 * f : 128 * f + 128] = high
                        work[pl.ds(768 + 256 * j + 32 * p, 32), 128 * f : 128 * f + 128] = low
                return inner

            lax.fori_loop(0, 8, fill, 0)
            term = mm(span_w[:, 0:1536], work[...]) + mm(
                span_w[:, 1536:2304], work[pl.ds(0, 768), :]
            )
            for f in range(5):
                part = term[:, 128 * f : 128 * f + 128].reshape(8, 4, 8, 128)
                old = out_reg[f, :, :, rows, half(h)]
                out_reg[f, :, :, rows, half(h)] = old - TIME_STEP * part
            return carry

        lax.fori_loop(0, 4, tile, 0)

    def finish(h, q):
        for offset in range(1, 8):
            giveback(h, q, offset).wait_recv()

        def join(p, carry):
            for f in range(5):
                fresh = out_reg[f, p, q, :, half(h)] - TIME_STEP * back[h, f, p, q]
                out_reg[f, p, q, :, half(h)] = fresh
                out_con[f, p, q, :, half(h)] = cur[h, f, p, q] + SECTION_GAIN * fresh
            return carry

        lax.fori_loop(0, 8, join, 0)

    for q in range(4):
        wall(1, q)
    for q in range(4):
        wall(0, q)
    span(1)
    span(0)
    for h in (1, 0):
        for q in range(4):
            finish(h, q)

    for offset in range(1, 8):
        stage_one(offset).wait_send()
    for offset in range(1, 16):
        stage_two(offset).wait_send()
    for h in (1, 0):
        for q in range(4):
            for offset in range(1, 8):
                forward(h, q, offset).wait_send()
                giveback(h, q, offset).wait_send()
            for side in range(2):
                beside(h, side, q).wait_send()
                if q < RELAYED:

                    @pl.when(relays[side])
                    def _(h=h, q=q, side=side):
                        onward(h, side, q).wait_send()


def store(con, reg, out_con, out_reg, sems):
    copies = [
        pltpu.make_async_copy(src.at[f], dst.at[f], sems.at[n, f])
        for f in range(5)
        for n, (src, dst) in enumerate(((con, out_con), (reg, out_reg)))
    ]
    for copy in copies:
        copy.start()
    for copy in copies:
        copy.wait()


def local(
    conserved,
    register,
    stream_blocks,
    wall_matrix,
    span_blocks,
    inflow_gain,
    source_block,
    source_column,
):
    shape = (5, 8, 4, 32, 256)
    anywhere = pl.BlockSpec(memory_space=pl.ANY)
    vmem = pl.BlockSpec(memory_space=pltpu.VMEM)
    dma = pltpu.SemaphoreType.DMA
    halved = (2, 5, 8, 4, 32, 128)
    new_conserved, new_register = pl.pallas_call(
        kernel,
        out_shape=[pltpu.VMEM(shape, F32)] * 2,
        in_specs=[
            anywhere,
            anywhere,
            vmem,
            vmem,
            vmem,
            pl.BlockSpec(memory_space=pltpu.SMEM),
            vmem,
            vmem,
        ],
        out_specs=[vmem, vmem],
        scratch_shapes=[
            pltpu.VMEM(halved, F32),
            pltpu.VMEM((2, 4, 5, 8, 32, 128), F32),
            pltpu.VMEM((2, 4, 5, 8, 32, 128), F32),
            pltpu.VMEM(halved, F32),
            pltpu.VMEM((2,) + halved, F32),
            pltpu.VMEM((2, RELAYED, 5, 2, 4, 32, 128), F32),
            pltpu.VMEM((1536, 640), BF16),
            pltpu.VMEM((640, 512), BF16),
            pltpu.VMEM((256, 768), BF16),
            pltpu.VMEM((256, 768), BF16),
            pltpu.VMEM((256, 2304), BF16),
            pltpu.VMEM((128, 1024), F32),
            pltpu.VMEM((8, 16, 128), F32),
            pltpu.VMEM((16, 8, 128), F32),
            pltpu.VMEM((16, 8, 128), F32),
            dma((4,)),
            dma((2, 4, 8)),
            dma((2, 4, 8)),
            dma((2, 4, 8)),
            dma((2, 4, 8)),
            dma((2, 2, 4)),
            dma((2, 2, 4)),
            dma((2, RELAYED)),
            dma((2, RELAYED)),
            dma((8,)),
            dma((8,)),
            dma((16,)),
            dma((16,)),
        ],
        compiler_params=pltpu.CompilerParams(
            collective_id=0, has_side_effects=True, vmem_limit_bytes=VMEM_MIB * 2**20
        ),
        name="section",
    )(
        conserved.reshape(shape),
        register.reshape(shape),
        stream_blocks,
        wall_matrix,
        span_blocks,
        inflow_gain,
        jnp.swapaxes(source_block, 1, 2),
        source_column,
    )
    new_conserved, new_register = pl.pallas_call(
        store,
        out_shape=[jax.ShapeDtypeStruct(shape, F32)] * 2,
        in_specs=[anywhere, anywhere],
        out_specs=[anywhere, anywhere],
        scratch_shapes=[dma((2, 5))],
        compiler_params=pltpu.CompilerParams(vmem_limit_bytes=2**20),
        name="store",
    )(new_conserved, new_register)
    return new_conserved.reshape(conserved.shape), new_register.reshape(register.shape)


def solution(mesh):
    split = P(None, "pz", "py", None)
    return jax.shard_map(
        local,
        mesh=mesh,
        in_specs=(split, split, P(), P(), P(), P(), P(), P()),
        out_specs=(split, split),
        check_vma=False,
    )
```
